256 devices in a mesh: blk: 16 (over z, core), head: 4 (over x), dp: 4 (over y).
Axes of the slice: x: 4, y: 4, z: 8, core: 2. Of those that a mesh axis runs over, the one named last changes fastest.
Arguments:
- hidden: bfloat16 [49152, 3072], P(('dp', 'blk', 'head')), parts along dimension 0, may hold values from -36 to 36
- qkv_weight: bfloat16 [3, 3072, 1536], P(None, None, 'head'), may hold values from -0.109375 to 0.109375
- qkv_bias: bfloat16 [3, 1536], P(None, 'head'), may hold values from -3 to 3
- norm_gains: float32 [2, 128], replicated, may hold values from 0.25 to 1.75
- tile_lists: int32 [128, 12], P('dp'), parts along dimension 0, may hold values from 0 to 31, as said below
- tile_counts: int32 [128], P('dp'), parts along dimension 0, may hold values from 1 to 12
Outputs:
- attended: bfloat16 [49152, 1536], P(('dp', 'blk', 'head')), parts along dimension 0
The draws below stay inside these ranges and needn't reach their ends.
There are 4 independent parts, one for each index of `dp`. The reference program is written for one: setup_inputs(seed, part) draws one part's arguments, and reference() takes and returns one part's arrays. A program takes and returns all parts, laid end to end along the dimension named above; an argument that names none is the same for every part. Nothing has to cross between parts.
Inputs may be any that keep to these rules, and one draw needn't show every extreme that they name: `tile_lists`: entries 0 to tile_counts[a] - 1 of row a name distinct tiles, tile a among them; later entries are arbitrary tile indices.
All inputs are finite; a program needn't handle non-finite values.
Results may differ from the reference program's by a relative error of at most 0.0034.
Values may be sent and summed in bfloat16 or wider, within the bound.
A program may use at most 64 MiB of HBM per device.

```python
import math
import jax
import jax.numpy as jnp
from jax import lax

D = 3072
HD = 128
HEADS = 12
TILE = 384
KMAX = 12
NTILES = 32
TOKENS = 12288


def window_lists(key):
    base = jax.random.fold_in(key, 7)
    key_reach, key_order, key_fill = jax.random.split(base, 3)
    tiles = jnp.arange(NTILES, dtype=jnp.int32)
    frame = tiles // 4
    row_pos = tiles // 2 % 2
    col_pos = tiles % 2
    reach = jax.random.randint(key_reach, (NTILES, 3), 0, 2)
    reach = jnp.where(tiles[:, None] == min(5, NTILES - 1), 1, reach)
    offs = jnp.arange(27, dtype=jnp.int32)
    step_f = offs // 9 - 1
    step_h = offs // 3 % 3 - 1
    step_w = offs % 3 - 1
    near_f = frame[:, None] + step_f[None, :]
    near_h = row_pos[:, None] + step_h[None, :]
    near_w = col_pos[:, None] + step_w[None, :]
    target = near_f * 4 + near_h * 2 + near_w
    valid = (jnp.abs(step_f)[None, :] <= reach[:, 0:1]) & (jnp.abs(step_h)[None, :] <= reach[:, 1:2]) & (jnp.abs(step_w)[None, :] <= reach[:, 2:3])
    valid = valid & (near_f >= 0) & (near_h >= 0) & (near_h < 2) & (near_w >= 0) & (near_w < 2) & (target < NTILES)
    noise = jax.random.randint(key_order, (NTILES, 27), 0, 1000)
    score = jnp.where(valid, 0, 1) * 100000 + noise * 32 + offs[None, :]
    order = jnp.argsort(score, axis=1, stable=True)[:, :KMAX]
    picked = jnp.take_along_axis(target, order, axis=1)
    picked_ok = jnp.take_along_axis(valid, order, axis=1)
    filler = jax.random.randint(key_fill, (NTILES, KMAX), 0, NTILES)
    lists = jnp.where(picked_ok, picked, filler).astype(jnp.int32)
    counts = jnp.sum(valid.astype(jnp.int32), axis=1).astype(jnp.int32)
    return (lists, counts)


def draw_tile_lists(key, part):
    return window_lists(key)[0]


def draw_tile_counts(key, part):
    return window_lists(key)[1]


def draw_hidden(key, part):
    key_base, key_rows, key_cols = jax.random.split(key, 3)
    low = math.log(0.3)
    high = math.log(3.0)
    row_scale = jnp.exp(jax.random.uniform(key_rows, (TOKENS, 1), jnp.float32, low, high))
    col_scale = jnp.exp(jax.random.uniform(key_cols, (1, D), jnp.float32, low, high))
    base = jnp.clip(jax.random.normal(key_base, (TOKENS, D), jnp.float32), -4.0, 4.0)
    return (base * row_scale * col_scale).astype(jnp.bfloat16)


def shard_levels(stream_key, shape, cuts, smallest, largest):
    def one(position, shards_of):
        steps = jax.random.uniform(jax.random.fold_in(jax.random.fold_in(stream_key, 6), position), (shards_of,), jnp.float32, smallest / len(cuts), largest / len(cuts))
        return jnp.repeat(jnp.exp(steps), shape[position] // shards_of).reshape((-1,) + (1,) * (len(shape) - position - 1))

    level = one(*cuts[0])
    for cut in cuts[1:]:
        level = level * one(*cut)
    return level


def bell_draw(key, extent, scale, limit, shards=(), kind=jnp.bfloat16):
    drawn = scale * jax.random.normal(key, extent, jnp.float32)
    if shards:
        drawn = drawn * shard_levels(key, extent, shards, -0.22, 0.18)
    return jnp.clip(drawn, -limit, limit).astype(kind)


def setup_inputs(seed: int = 0, part: int = 0) -> dict:
    arg_keys = jax.random.split(jax.random.key(seed), 7)
    part_splits = jax.random.split(jax.random.fold_in(arg_keys[6], part), 7)
    return {
        "hidden": draw_hidden(jax.random.fold_in(jax.random.fold_in(arg_keys[6], part), 71), part),
        "qkv_weight": bell_draw(arg_keys[1], (3, D, HEADS * HD), D ** -0.5, 0.109375, ((2, 4),)),
        "qkv_bias": bell_draw(arg_keys[2], (3, HEADS * HD), 0.5, 3.0, ((1, 4),)),
        "norm_gains": jnp.clip(1.0 + 0.15 * jax.random.normal(arg_keys[3], (2, HD), jnp.float32), 0.25, 1.75),
        "tile_lists": draw_tile_lists(jax.random.fold_in(jax.random.fold_in(arg_keys[6], part), 71), part),
        "tile_counts": draw_tile_counts(jax.random.fold_in(jax.random.fold_in(arg_keys[6], part), 71), part),
    }


def norm_heads(values, gain):
    rows = values.shape[0]
    split = values.reshape(rows, HEADS, HD)
    mean_sq = lax.optimization_barrier(jnp.mean(split * split, axis=-1, keepdims=True))
    return (split * lax.rsqrt(mean_sq + 1e-06) * gain).reshape(rows, HEADS * HD)

def reference(hidden, qkv_weight, qkv_bias, norm_gains, tile_lists, tile_counts):
    projected = [jnp.dot(hidden, qkv_weight[j], preferred_element_type=jnp.float32) + qkv_bias[j].astype(jnp.float32) for j in range(3)]
    query = norm_heads(projected[0], norm_gains[0]).astype(jnp.bfloat16)
    keys = norm_heads(projected[1], norm_gains[1]).astype(jnp.bfloat16)
    values = projected[2].astype(jnp.bfloat16)
    query_tiles = query.reshape(NTILES, TILE, HEADS, HD)
    key_tiles = keys.reshape(NTILES, TILE, HEADS, HD)
    value_tiles = values.reshape(NTILES, TILE, HEADS, HD)
    scale = HD ** (-0.5)

    def one_tile(index):
        chosen = tile_lists[index]
        live = jnp.arange(KMAX, dtype=jnp.int32) < tile_counts[index]
        keep = jnp.repeat(live, TILE)
        near_keys = key_tiles[chosen].astype(jnp.float32).reshape(KMAX * TILE, HEADS, HD)
        near_values = value_tiles[chosen].astype(jnp.float32).reshape(KMAX * TILE, HEADS, HD)
        own = query_tiles[index].astype(jnp.float32)
        score = jnp.einsum('qhd,khd->hqk', own, near_keys, precision=lax.Precision.HIGHEST) * scale
        weights = jnp.where(keep[None, None, :], jnp.exp(score), jnp.float32(0.0))
        total = lax.optimization_barrier(jnp.sum(weights, axis=-1))
        rounded = weights.astype(jnp.bfloat16).astype(jnp.float32)
        numer = jnp.einsum('hqk,khd->qhd', rounded, near_values, precision=lax.Precision.HIGHEST)
        return (numer / total.T[:, :, None]).reshape(TILE, HEADS * HD).astype(jnp.bfloat16)
    result = lax.map(one_tile, jnp.arange(NTILES, dtype=jnp.int32))
    return result.reshape(TOKENS, HEADS * HD)
```

```python
import functools

import jax
import jax.numpy as jnp
from jax import lax
from jax.experimental import pallas as pl
from jax.experimental.pallas import tpu as pltpu
from jax.sharding import PartitionSpec as P

HD = 128
TILE = 384
MESH = pl.DeviceIdType.MESH


def kernel(
    sizes,
    hidden, weight, bias, gains, lists, counts,
    out, q_out, kv_out, flag_out,
    hid, wv, qb, kv, acc, ob, flags, mask,
    own_sem, w_sem, hs_sem, hr_sem, ks_sem, kr_sem, os_sem, or_sem, fs_sem, fr_sem, x_sem,
):
    n_blk, n_dp, heads, slots, n_tiles = sizes
    chunk = hid.shape[1]
    half = chunk // 2
    width = heads * HD
    b = lax.axis_index("blk")
    h = lax.axis_index("head")
    d = lax.axis_index("dp")
    c = lax.rem(b, 2)
    z = lax.div(b, 2)
    n_z = n_blk // 2
    right = lax.rem(h + 1, 4)
    opp = lax.rem(h + 2, 4)
    left = lax.rem(h + 3, 4)
    hb = lax.rem(h, 2)
    t0 = lax.div(h, 2)
    mate = h + 1 - 2 * hb
    other = lax.rem(h + 3 + 2 * hb, 4)
    partner = b + 1 - 2 * c
    up = lax.rem(b + 2, n_blk)
    down = lax.rem(b + n_blk - 2, n_blk)
    dps = [lax.rem(d + i, n_dp) for i in range(1, n_dp)]

    own_in = pltpu.make_async_copy(hidden, hid.at[h], own_sem)
    own_in.start()
    w_in = [pltpu.make_async_copy(weight.at[j], wv.at[j], w_sem.at[j]) for j in (1, 2, 0)]
    for copy in w_in:
        copy.start()

    barrier = pltpu.get_barrier_semaphore()
    for p in (right, opp, left):
        pl.semaphore_signal(barrier, inc=1, device_id={"head": p}, device_id_type=MESH)
    for p in (partner, up, down):
        pl.semaphore_signal(barrier, inc=1, device_id={"blk": p}, device_id_type=MESH)
    for p in dps:
        pl.semaphore_signal(barrier, inc=1, device_id={"dp": p}, device_id_type=MESH)
    pl.semaphore_wait(barrier, 6 + len(dps))

    def hid_send(src, slot, start, to, k):
        return pltpu.make_async_remote_copy(
            src_ref=src,
            dst_ref=hid.at[slot, pl.ds(start, half)],
            send_sem=hs_sem.at[k],
            recv_sem=hr_sem.at[k],
            device_id={"head": to},
            device_id_type=MESH,
        )

    top = hidden.at[pl.ds(0, half)]
    bottom = hidden.at[pl.ds(half, half)]
    hops = [
        hid_send(top, h, 0, right, 0),
        hid_send(bottom, h, half, left, 3),
        hid_send(bottom, h, half, right, 1),
        hid_send(top, h, 0, left, 4),
        hid_send(hid.at[left, pl.ds(0, half)], left, 0, right, 2),
        hid_send(hid.at[right, pl.ds(half, half)], right, half, left, 5),
    ]
    for copy in hops[:4]:
        copy.start()

    def hid_wait(slot, start, k):
        part = hid.at[slot, pl.ds(start, half)]
        pltpu.make_async_copy(part, part, hr_sem.at[k]).wait()

    def rows_of(core, part):
        return pl.ds(pl.multiple_of(core * TILE + part * chunk, chunk), chunk)

    def kv_copy(src_f, dst_f, kt, part, to, kind, stage):
        rows = rows_of(c, part)
        return pltpu.make_async_remote_copy(
            src_ref=kv.at[src_f, kt, rows],
            dst_ref=kv.at[dst_f, kt, rows],
            send_sem=ks_sem.at[kind, stage],
            recv_sem=kr_sem.at[kind, stage],
            device_id={"blk": to},
            device_id_type=MESH,
        )

    def kv_wait(f, kt, core, part, kind, stage):
        ref = kv.at[f, kt, rows_of(core, part)]
        pltpu.make_async_copy(ref, ref, kr_sem.at[kind, stage]).wait()

    part_of = [hb, 1 - hb, 1 - hb, hb]
    slot_of = [h, mate, other, opp]

    def project(stage, first):
        kt, part, slot = stage // 2, part_of[stage], slot_of[stage]
        x = hid[slot]
        for n, j in enumerate((1, 2, 0)):
            if first:
                w_in[n].wait()
            made = jnp.dot(x, wv[j], preferred_element_type=jnp.float32)
            made = made + bias[pl.ds(j, 1), :].astype(jnp.float32)
            for g in range(heads):
                cols = slice(g * HD, (g + 1) * HD)
                piece = made[:, cols]
                if j < 2:
                    mean_sq = jnp.mean(piece * piece, axis=-1, keepdims=True)
                    piece = piece * lax.rsqrt(mean_sq + 1e-06) * gains[pl.ds(j, 1), :]
                piece = piece.astype(jnp.bfloat16)
                if j == 0:
                    rows = pl.ds(pl.multiple_of(part * chunk, chunk), chunk)
                    qb[kt, rows, cols] = piece
                else:
                    off = (j - 1) * width + g * HD
                    kv[1, kt, rows_of(c, part), off : off + HD] = piece
        kv_copy(1, 2, kt, part, down, 2, stage).start()
        kv_copy(1, 0, kt, part, up, 1, stage).start()
        kv_copy(1, 1, kt, part, partner, 0, stage).start()

    def relay(stage):
        kt, part = stage // 2, part_of[stage]
        kv_wait(0, kt, c, part, 1, stage)
        kv_copy(0, 0, kt, part, partner, 3, stage).start()
        kv_wait(2, kt, c, part, 2, stage)
        kv_copy(2, 2, kt, part, partner, 4, stage).start()

    def near(stage):
        kv_wait(1, stage // 2, 1 - c, part_of[stage], 0, stage)

    def far(stage):
        kv_wait(0, stage // 2, 1 - c, part_of[stage], 3, stage)
        kv_wait(2, stage // 2, 1 - c, part_of[stage], 4, stage)

    own_in.wait()
    project(0, True)

    def check_row(t, bad):
        n = counts[t]
        for s in range(slots):
            gap = lax.rem(lists[t, s] // 4 - t // 4 + n_z, n_z)
            far_one = jnp.where((gap > 1) & (gap < n_z - 1) & (s < n), 1, 0)
            bad = jnp.maximum(bad, far_one)
        return bad

    bad = lax.fori_loop(0, n_tiles, check_row, jnp.int32(0))
    flags[d] = jnp.full(flags.shape[1:], bad, jnp.int32)

    def mask_entry(i, carry):
        q = i // 12
        f = lax.rem(i // 4, 3)
        kt = lax.rem(i // 2, 2)
        core = lax.rem(i, 2)
        row = 2 * b + lax.rem(t0 + q, 2)
        tile = 4 * lax.rem(z + f + n_z - 1, n_z) + 2 * core + lax.rem(t0 + kt, 2)
        n = counts[row]
        hit = jnp.int32(0)
        for s in range(slots):
            hit = jnp.maximum(hit, jnp.where((lists[row, s] == tile) & (s < n), 1, 0))
        mask[i] = hit.astype(jnp.float32)
        return carry

    lax.fori_loop(0, 24, mask_entry, 0)

    def flag_send(i, to):
        return pltpu.make_async_remote_copy(
            src_ref=flags.at[d],
            dst_ref=flags.at[d],
            send_sem=fs_sem.at[i],
            recv_sem=fr_sem.at[i],
            device_id={"dp": to},
            device_id_type=MESH,
        )

    flag_sends = [flag_send(i, p) for i, p in enumerate(dps)]
    for copy in flag_sends:
        copy.start()

    acc[...] = jnp.zeros_like(acc)

    hid_wait(left, 0, 0)
    hops[4].start()
    hid_wait(right, half, 3)
    hops[5].start()
    relay(0)
    for i, p in enumerate(dps):
        src = lax.rem(d + n_dp - 1 - i, n_dp)
        ref = flags.at[src]
        pltpu.make_async_copy(ref, ref, fr_sem.at[i]).wait()
    flag_out[...] = jnp.max(flags[...], axis=0)
    hid_wait(left, half, 1)
    hid_wait(right, 0, 4)
    project(1, False)
    project(2, False)
    near(0)
    near(1)

    def attend(q, f, kt):
        base = q * 12 + f * 4 + kt * 2
        live = jnp.concatenate(
            [
                jnp.full((TILE, HD), mask[base], jnp.float32),
                jnp.full((TILE, HD), mask[base + 1], jnp.float32),
            ],
            axis=0,
        ).astype(jnp.bfloat16)
        for g in range(heads):
            qh = qb[q, :, g * HD : (g + 1) * HD]
            kh = kv[f, kt, :, g * HD : (g + 1) * HD]
            vh = kv[f, kt, :, width + g * HD : width + (g + 1) * HD]
            score = lax.dot_general(
                qh, kh, (((1,), (1,)), ((), ())), preferred_element_type=jnp.float32
            )
            w = jnp.exp(score * HD ** (-0.5)).astype(jnp.bfloat16)
            ext = jnp.concatenate([vh * live, live], axis=1)
            acc[q, g] += jnp.dot(w, ext, preferred_element_type=jnp.float32)

    def finish(q):
        for g in range(heads):
            full = acc[q, g]
            ob[q, :, g * HD : (g + 1) * HD] = (full[:, :HD] / full[:, HD:]).astype(jnp.bfloat16)

    cols = pl.ds(pl.multiple_of(h * width, width), width)

    def out_send(q, part, to, k):
        return pltpu.make_async_remote_copy(
            src_ref=ob.at[q, pl.ds(pl.multiple_of(part * chunk, chunk), chunk)],
            dst_ref=out.at[:, cols],
            send_sem=os_sem.at[k],
            recv_sem=or_sem.at[k],
            device_id={"head": to},
            device_id_type=MESH,
        )

    out_sends = [
        out_send(1, hb, opp, 0),
        out_send(1, 1 - hb, other, 1),
        out_send(0, 1 - hb, mate, 2),
    ]
    own_out = pltpu.make_async_copy(
        ob.at[0, pl.ds(pl.multiple_of(hb * chunk, chunk), chunk)], out.at[:, cols], own_sem
    )

    def first_half(i, carry):
        j = lax.rem(i, 3)

        @pl.when(i == 1)
        def _():
            relay(1)
            far(0)
            far(1)

        @pl.when(i == 3)
        def _():
            hid_wait(opp, 0, 2)
            hid_wait(opp, half, 5)
            project(3, False)
            relay(2)

        attend(lax.div(i, 3), lax.rem(2 * j + 1, 3), 0)
        return carry

    lax.fori_loop(0, 6, first_half, 0)
    near(2)
    near(3)
    keep = [
        pltpu.make_async_copy(qb, q_out, x_sem.at[0]),
        pltpu.make_async_copy(kv.at[1, :, pl.ds(pl.multiple_of(c * TILE, TILE), TILE)], kv_out, x_sem.at[1]),
    ]
    for copy in keep:
        copy.start()

    def second_half(i, carry):
        g = lax.div(i, 2)
        new = lax.div(g + 1, 2)

        @pl.when(i == 2)
        def _():
            relay(3)
            far(2)
            far(3)

        attend(
            (1 - new) * (1 - i) + new * (2 - g),
            1 - new + new * 2 * lax.rem(i, 2),
            1,
        )

        @pl.when(i == 3)
        def _():
            finish(1)
            out_sends[0].start()
            out_sends[1].start()

        return carry

    lax.fori_loop(0, 6, second_half, 0)
    finish(0)
    out_sends[2].start()
    own_out.start()

    for copy in hops:
        copy.wait_send()
    for stage in range(4):
        kt, part = stage // 2, part_of[stage]
        kv_copy(1, 1, kt, part, partner, 0, stage).wait_send()
        kv_copy(1, 0, kt, part, up, 1, stage).wait_send()
        kv_copy(1, 2, kt, part, down, 2, stage).wait_send()
        kv_copy(0, 0, kt, part, partner, 3, stage).wait_send()
        kv_copy(2, 2, kt, part, partner, 4, stage).wait_send()
    for copy in flag_sends:
        copy.wait_send()
    for copy in keep:
        copy.wait()
    own_out.wait()
    for copy in out_sends:
        copy.wait_send()
    for k, src in enumerate((opp, other, mate)):
        ref = out.at[:, pl.ds(pl.multiple_of(src * width, width), width)]
        pltpu.make_async_copy(ref, ref, or_sem.at[k]).wait()


def window_attention(hidden, weight, bias, gains, lists, counts):
    n_blk = lax.axis_size("blk")
    n_dp = lax.axis_size("dp")
    chunk, depth = hidden.shape
    width = weight.shape[2]
    heads = width // HD
    n_tiles, slots = lists.shape
    sizes = (n_blk, n_dp, heads, slots, n_tiles)
    hbm = pl.BlockSpec(memory_space=pl.ANY)
    vmem = pl.BlockSpec(memory_space=pltpu.VMEM)
    smem = pl.BlockSpec(memory_space=pltpu.SMEM)
    dma = pltpu.SemaphoreType.DMA
    return pl.pallas_call(
        functools.partial(kernel, sizes),
        out_shape=(
            jax.ShapeDtypeStruct((chunk, 4 * width), jnp.bfloat16),
            jax.ShapeDtypeStruct((2, TILE, width), jnp.bfloat16),
            jax.ShapeDtypeStruct((2, TILE, 2 * width), jnp.bfloat16),
            jax.ShapeDtypeStruct((8, 128), jnp.int32),
        ),
        in_specs=[hbm, hbm, vmem, vmem, smem, smem],
        out_specs=(hbm, hbm, hbm, vmem),
        scratch_shapes=[
            pltpu.VMEM((4, chunk, depth), jnp.bfloat16),
            pltpu.VMEM((3, depth, width), jnp.bfloat16),
            pltpu.VMEM((2, TILE, width), jnp.bfloat16),
            pltpu.VMEM((3, 2, 2 * TILE, 2 * width), jnp.bfloat16),
            pltpu.VMEM((2, heads, TILE, 2 * HD), jnp.float32),
            pltpu.VMEM((2, TILE, width), jnp.bfloat16),
            pltpu.VMEM((n_dp, 8, 128), jnp.int32),
            pltpu.SMEM((24,), jnp.float32),
            dma,
            dma((3,)),
            dma((6,)),
            dma((6,)),
            dma((5, 4)),
            dma((5, 4)),
            dma((3,)),
            dma((3,)),
            dma((n_dp - 1,)),
            dma((n_dp - 1,)),
            dma((2,)),
        ],
        compiler_params=pltpu.CompilerParams(
            collective_id=0, has_side_effects=True, vmem_limit_bytes=60 * 1024 * 1024
        ),
    )(hidden, weight, bias, gains, lists, counts)


def any_lists(query, key_value, tile_lists, tile_counts):
    n_blk = lax.axis_size("blk")
    place = lax.axis_index("blk")
    t0 = lax.axis_index("head") // 2
    width = query.shape[2]
    heads = width // HD
    rows = 2 * TILE

    def in_order(tiles):
        return jnp.where(t0 == 0, tiles, tiles[::-1]).reshape(rows, -1)

    query = in_order(query).reshape(rows, heads, HD)
    current = in_order(key_value)
    lists = lax.dynamic_slice_in_dim(tile_lists, place * 2, 2, 0)
    counts = lax.dynamic_slice_in_dim(tile_counts, place * 2, 2, 0)
    live = jnp.arange(lists.shape[1], dtype=jnp.int32)[None, :] < counts[:, None]
    route = [(i, (i - 1) % n_blk) for i in range(n_blk)]

    def turn(step, carry):
        total, numer, block = carry
        key_tile = 2 * ((place + step) % n_blk) + jnp.arange(rows, dtype=jnp.int32) // TILE
        hits = (lists[:, :, None] == key_tile[None, None, :]) & live[:, :, None]
        mask = jnp.repeat(jnp.any(hits, axis=1), TILE, axis=0)
        keys = block[:, :width].reshape(rows, heads, HD)
        values = block[:, width:].reshape(rows, heads, HD)
        score = jnp.einsum("qhd,khd->hqk", query, keys, preferred_element_type=jnp.float32)
        w = jnp.where(mask[None], jnp.exp(score * HD ** (-0.5)), jnp.float32(0.0))
        total = total + jnp.sum(w, axis=-1)
        numer = numer + jnp.einsum(
            "hqk,khd->hqd", w.astype(jnp.bfloat16), values, preferred_element_type=jnp.float32
        )
        return (total, numer, lax.ppermute(block, "blk", route))

    total, numer, current = lax.fori_loop(
        0,
        n_blk,
        turn,
        (
            jnp.zeros((heads, rows), jnp.float32),
            jnp.zeros((heads, rows, HD), jnp.float32),
            current,
        ),
    )
    attended = (numer / total[:, :, None]).transpose(1, 0, 2).reshape(rows, width)
    return lax.all_to_all(
        attended.astype(jnp.bfloat16), "head", split_axis=0, concat_axis=1, tiled=True
    )


def shards(hidden, qkv_weight, qkv_bias, norm_gains, tile_lists, tile_counts):
    out, query, key_value, flag = window_attention(
        hidden, qkv_weight, qkv_bias, norm_gains, tile_lists, tile_counts
    )
    return lax.cond(
        flag[0, 0] > 0,
        lambda: any_lists(query, key_value, tile_lists, tile_counts),
        lambda: out,
    )


def solution(mesh):
    return jax.shard_map(
        shards,
        mesh=mesh,
        in_specs=(
            P(("dp", "blk", "head"), None),
            P(None, None, "head"),
            P(None, "head"),
            P(),
            P("dp", None),
            P("dp"),
        ),
        out_specs=P(("dp", "blk", "head"), None),
        check_vma=False,
    )
```

```python
import functools

import jax
import jax.numpy as jnp
from jax import lax
from jax.experimental import pallas as pl
from jax.experimental.pallas import tpu as pltpu
from jax.sharding import PartitionSpec as P

HD = 128
TILE = 384
MESH = pl.DeviceIdType.MESH


def kernel(
    sizes,
    hidden, weight, bias, gains, lists, counts,
    out, q_out, kv_out, flag_out,
    hid, wv, qb, kv, acc, ob, passing, flags, mask,
    own_sem, w_sem, hs_sem, hr_sem, ks_sem, kr_sem, os_sem, or_sem, fs_sem, fr_sem, x_sem,
):
    n_blk, n_dp, heads, slots, n_tiles = sizes
    chunk = hid.shape[1]
    half = chunk // 2
    quarter = chunk // 4
    width = heads * HD
    b = lax.axis_index("blk")
    h = lax.axis_index("head")
    d = lax.axis_index("dp")
    c = lax.rem(b, 2)
    z = lax.div(b, 2)
    n_z = n_blk // 2
    right = lax.rem(h + 1, 4)
    opp = lax.rem(h + 2, 4)
    left = lax.rem(h + 3, 4)
    hb = lax.rem(h, 2)
    t0 = lax.div(h, 2)
    mate = h + 1 - 2 * hb
    other = lax.rem(h + 3 + 2 * hb, 4)
    partner = b + 1 - 2 * c
    up = lax.rem(b + 2, n_blk)
    down = lax.rem(b + n_blk - 2, n_blk)
    dps = [lax.rem(d + i, n_dp) for i in range(1, n_dp)]

    own_in = pltpu.make_async_copy(hidden, hid.at[0], own_sem)
    own_in.start()
    w_in = [pltpu.make_async_copy(weight.at[j], wv.at[j], w_sem.at[j]) for j in (1, 2, 0)]
    for copy in w_in:
        copy.start()

    barrier = pltpu.get_barrier_semaphore()
    for p in (right, opp, left):
        pl.semaphore_signal(barrier, inc=1, device_id={"head": p}, device_id_type=MESH)
    for p in (partner, up, down):
        pl.semaphore_signal(barrier, inc=1, device_id={"blk": p}, device_id_type=MESH)
    for p in dps:
        pl.semaphore_signal(barrier, inc=1, device_id={"dp": p}, device_id_type=MESH)
    pl.semaphore_wait(barrier, 6 + len(dps))

    def hid_send(src, slot, start, rows, to, k):
        return pltpu.make_async_remote_copy(
            src_ref=src.at[pl.ds(start, rows)],
            dst_ref=hid.at[slot, pl.ds(start, rows)],
            send_sem=hs_sem.at[k],
            recv_sem=hr_sem.at[k],
            device_id={"head": to},
            device_id_type=MESH,
        )

    hops = [
        hid_send(hidden, 1, 0, half, right, 0),
        hid_send(hidden, 2, half, half, left, 4),
        hid_send(hidden, 1, half, half, right, 1),
        hid_send(hidden, 2, 0, half, left, 5),
        hid_send(hid.at[1], 3, 0, quarter, right, 2),
        hid_send(hid.at[2], 3, 3 * quarter, quarter, left, 6),
        hid_send(hid.at[1], 3, quarter, quarter, right, 3),
        hid_send(hid.at[2], 3, 2 * quarter, quarter, left, 7),
    ]
    for copy in hops[:4]:
        copy.start()

    def hid_wait(slot, start, rows, k):
        part = hid.at[slot, pl.ds(start, rows)]
        pltpu.make_async_copy(part, part, hr_sem.at[k]).wait()

    mate_left = hb
    left_block = 2 - mate_left
    right_block = 1 + mate_left
    batches = [
        (0, chunk, [(0, 0, chunk, 0, 0)]),
        (2 * chunk, chunk, [(1, 0, half, left_block, 0), (2, half, half, right_block, half)]),
        (4 * chunk, chunk, [(1, half, half, left_block, half), (2, 0, half, right_block, 0)]),
        (6 * chunk, half, [(3, 0, quarter, 3, 0), (3, 3 * quarter, quarter, 3, 3 * quarter)]),
        (7 * chunk, half, [(3, quarter, half, 3, quarter)]),
    ]

    def key_rows(n, core):
        first, rows, _ = batches[n]
        return pl.ds(pl.multiple_of(first + core * rows, rows), rows)

    def kv_copy(src_f, dst_f, n, to, kind):
        rows = key_rows(n, c)
        return pltpu.make_async_remote_copy(
            src_ref=kv.at[src_f, rows],
            dst_ref=kv.at[dst_f, rows],
            send_sem=ks_sem.at[kind, n],
            recv_sem=kr_sem.at[kind, n],
            device_id={"blk": to},
            device_id_type=MESH,
        )

    def kv_wait(f, n, core, kind):
        ref = kv.at[f, key_rows(n, core)]
        pltpu.make_async_copy(ref, ref, kr_sem.at[kind, n]).wait()

    def project(n):
        _, _, pieces = batches[n]
        parts = [hid[slot, start : start + rows] for slot, start, rows, _, _ in pieces]
        x = parts[0] if len(parts) == 1 else jnp.concatenate(parts, axis=0)
        for order, j in enumerate((1, 2, 0)):
            if n == 0:
                w_in[order].wait()
            made = jnp.dot(x, wv[j], preferred_element_type=jnp.float32)
            made = made + bias[pl.ds(j, 1), :].astype(jnp.float32)
            for g in range(heads):
                cols = slice(g * HD, (g + 1) * HD)
                piece = made[:, cols]
                if j < 2:
                    mean_sq = jnp.mean(piece * piece, axis=-1, keepdims=True)
                    piece = piece * lax.rsqrt(mean_sq + 1e-06) * gains[pl.ds(j, 1), :]
                piece = piece.astype(jnp.bfloat16)
                if j == 0:
                    at = 0
                    for _, _, rows, block, start in pieces:
                        qb[block, start : start + rows, cols] = piece[at : at + rows]
                        at += rows
                else:
                    off = (j - 1) * width + g * HD
                    kv[1, key_rows(n, c), off : off + HD] = piece
            if j == 2:
                kv_copy(1, 2, n, down, 2).start()
                kv_copy(1, 0, n, up, 1).start()
                kv_copy(1, 1, n, partner, 0).start()

    def relay(n):
        kv_wait(0, n, c, 1)
        kv_copy(0, 0, n, partner, 3).start()
        kv_wait(2, n, c, 2)
        kv_copy(2, 2, n, partner, 4).start()

    def near(n):
        kv_wait(1, n, 1 - c, 0)

    def far(n):
        kv_wait(0, n, 1 - c, 3)
        kv_wait(2, n, 1 - c, 4)

    own_in.wait()
    project(0)

    def check_row(t, bad):
        n = counts[t]
        for s in range(slots):
            gap = lax.rem(lists[s, t] // 4 - t // 4 + n_z, n_z)
            far_one = jnp.where((gap > 1) & (gap < n_z - 1) & (s < n), 1, 0)
            bad = jnp.maximum(bad, far_one)
        return bad

    bad = lax.fori_loop(0, n_tiles, check_row, jnp.int32(0))
    flags[d] = jnp.full(flags.shape[1:], bad, jnp.int32)

    def mask_entry(i, carry):
        q = i // 12
        f = lax.rem(i // 4, 3)
        kt = lax.rem(i // 2, 2)
        core = lax.rem(i, 2)
        row = 2 * b + lax.rem(t0 + q, 2)
        tile = 4 * lax.rem(z + f + n_z - 1, n_z) + 2 * core + lax.rem(t0 + kt, 2)
        n = counts[row]
        hit = jnp.int32(0)
        for s in range(slots):
            hit = jnp.maximum(hit, jnp.where((lists[s, row] == tile) & (s < n), 1, 0))
        mask[i] = hit.astype(jnp.float32)
        return carry

    lax.fori_loop(0, 24, mask_entry, 0)

    def flag_send(i, to):
        return pltpu.make_async_remote_copy(
            src_ref=flags.at[d],
            dst_ref=flags.at[d],
            send_sem=fs_sem.at[i],
            recv_sem=fr_sem.at[i],
            device_id={"dp": to},
            device_id_type=MESH,
        )

    flag_sends = [flag_send(i, p) for i, p in enumerate(dps)]
    for copy in flag_sends:
        copy.start()

    acc[...] = jnp.zeros_like(acc)

    segments = {
        0: [(chunk, 0, 0), (chunk, 0, 1)],
        1: [(half, 1 - mate_left, 0), (half, mate_left, 0), (half, 1 - mate_left, 1), (half, mate_left, 1)],
        3: [(half, 1, 0), (half, 1, 1)],
    }
    segments[2] = segments[1]
    segments[4] = segments[3]

    def attend(block, tile, f, group):
        base = tile * 12 + f * 4
        live = jnp.concatenate(
            [
                jnp.full((rows, HD), mask[base + kt * 2 + core], jnp.float32)
                for n in group
                for rows, kt, core in segments[n]
            ],
            axis=0,
        ).astype(jnp.bfloat16)
        keys = slice(batches[group[0]][0], batches[group[0]][0] + live.shape[0])
        for g in range(heads):
            qh = qb[block, :, g * HD : (g + 1) * HD]
            kh = kv[f, keys, g * HD : (g + 1) * HD]
            vh = kv[f, keys, width + g * HD : width + (g + 1) * HD]
            score = lax.dot_general(
                qh, kh, (((1,), (1,)), ((), ())), preferred_element_type=jnp.float32
            )
            w = jnp.exp(score * HD ** (-0.5)).astype(jnp.bfloat16)
            ext = jnp.concatenate([vh * live, live], axis=1)
            acc[block, g] += jnp.dot(w, ext, preferred_element_type=jnp.float32)

    def finish(block):
        for g in range(heads):
            full = acc[block, g]
            ob[block, :, g * HD : (g + 1) * HD] = (full[:, :HD] / full[:, HD:]).astype(jnp.bfloat16)

    def columns(p):
        return pl.ds(pl.multiple_of(p * width, width), width)

    def out_send(src, dst, to, k):
        return pltpu.make_async_remote_copy(
            src_ref=src,
            dst_ref=dst,
            send_sem=os_sem.at[k],
            recv_sem=or_sem.at[k],
            device_id={"head": to},
            device_id_type=MESH,
        )

    upper, lower = pl.ds(0, half), pl.ds(half, half)
    out_sends = [
        out_send(ob.at[3, upper], passing.at[0], right, 0),
        out_send(ob.at[3, lower], passing.at[1], left, 1),
        out_send(ob.at[2], out.at[:, columns(h)], other, 2),
        out_send(ob.at[1], out.at[:, columns(h)], mate, 3),
        out_send(passing.at[0], out.at[upper, columns(left)], right, 4),
        out_send(passing.at[1], out.at[lower, columns(right)], left, 5),
    ]
    own_out = pltpu.make_async_copy(ob.at[0], out.at[:, columns(h)], own_sem)

    hid_wait(1, 0, half, 0)
    hops[4].start()
    hops[6].start()
    hid_wait(2, half, half, 4)
    hops[5].start()
    hops[7].start()
    relay(0)
    project(1)
    for i in range(n_dp - 1):
        src = lax.rem(d + n_dp - 1 - i, n_dp)
        ref = flags.at[src]
        pltpu.make_async_copy(ref, ref, fr_sem.at[i]).wait()
    flag_out[...] = jnp.max(flags[:, 0:1, 0:1], axis=0)
    near(0)
    near(1)

    def own_first(i, carry):
        @pl.when(i == 1)
        def _():
            relay(1)
            far(0)
            far(1)

        attend(0, 0, lax.rem(2 * i + 1, 3), (0, 1))
        return carry

    lax.fori_loop(0, 3, own_first, 0)
    hid_wait(1, half, half, 1)
    hid_wait(2, 0, half, 5)
    project(2)

    def neighbours_first(i, carry):
        block = 1 + lax.div(i, 3)
        attend(block, lax.div(block, 2), lax.rem(i, 3), (0, 1))
        return carry

    lax.fori_loop(0, 6, neighbours_first, 0)
    hid_wait(3, 0, quarter, 2)
    hid_wait(3, 3 * quarter, quarter, 6)
    project(3)
    relay(2)
    near(2)
    near(3)

    def own_second(i, carry):
        attend(i, lax.div(i, 2), 1, (2, 3))
        return carry

    lax.fori_loop(0, 3, own_second, 0)
    relay(3)
    hid_wait(3, quarter, quarter, 3)
    hid_wait(3, 2 * quarter, quarter, 7)
    project(4)

    def opposite_first(i, carry):
        attend(3, 1, i, (0, 1))
        return carry

    lax.fori_loop(0, 3, opposite_first, 0)
    keep = [pltpu.make_async_copy(qb, q_out, x_sem.at[5])]
    at = 0
    for n, (_, rows, _) in enumerate(batches):
        keep.append(pltpu.make_async_copy(kv.at[1, key_rows(n, c)], kv_out.at[pl.ds(at, rows)], x_sem.at[n]))
        at += rows
    for copy in keep:
        copy.start()
    far(2)
    far(3)

    def second(i, carry):
        new = lax.div(i + 8, 9)
        block = 3 - new * lax.div(i + 1 - 2 * new + (1 - new), 2)
        attend(block, lax.div(block, 2), (1 - new) + new * 2 * lax.rem(i, 2), (2, 3))
        return carry

    lax.fori_loop(0, 9, second, 0)
    relay(4)
    near(4)

    def last(i, carry):
        new = lax.div(i + 8, 12)

        @pl.when(i == 4)
        def _():
            far(4)

        block = (1 - new) * i + new * (5 - lax.div(i, 2))
        attend(block, lax.div(block, 2), (1 - new) + new * 2 * lax.rem(i, 2), (4,))

        @pl.when((i >= 4) & (lax.rem(i, 2) == 1))
        def _():
            finish(block)

        @pl.when(i == 5)
        def _():
            out_sends[0].start()
            out_sends[1].start()

        @pl.when(i == 7)
        def _():
            out_sends[2].start()

        @pl.when(i == 9)
        def _():
            out_sends[3].start()

        return carry

    lax.fori_loop(0, 12, last, 0)
    own_out.start()
    for k in range(2):
        ref = passing.at[k]
        pltpu.make_async_copy(ref, ref, or_sem.at[k]).wait()
        out_sends[4 + k].start()

    for copy in hops:
        copy.wait_send()
    for n in range(5):
        kv_copy(1, 1, n, partner, 0).wait_send()
        kv_copy(1, 0, n, up, 1).wait_send()
        kv_copy(1, 2, n, down, 2).wait_send()
        kv_copy(0, 0, n, partner, 3).wait_send()
        kv_copy(2, 2, n, partner, 4).wait_send()
    for copy in flag_sends:
        copy.wait_send()
    for copy in keep:
        copy.wait()
    own_out.wait()
    for copy in out_sends:
        copy.wait_send()
    for k, ref in (
        (2, out.at[:, columns(other)]),
        (3, out.at[:, columns(mate)]),
        (4, out.at[upper, columns(opp)]),
        (5, out.at[lower, columns(opp)]),
    ):
        pltpu.make_async_copy(ref, ref, or_sem.at[k]).wait()


def window_attention(hidden, weight, bias, gains, lists, counts):
    n_blk = lax.axis_size("blk")
    n_dp = lax.axis_size("dp")
    chunk, depth = hidden.shape
    width = weight.shape[2]
    heads = width // HD
    slots, n_tiles = lists.shape
    sizes = (n_blk, n_dp, heads, slots, n_tiles)
    hbm = pl.BlockSpec(memory_space=pl.ANY)
    vmem = pl.BlockSpec(memory_space=pltpu.VMEM)
    smem = pl.BlockSpec(memory_space=pltpu.SMEM)
    dma = pltpu.SemaphoreType.DMA
    return pl.pallas_call(
        functools.partial(kernel, sizes),
        out_shape=(
            jax.ShapeDtypeStruct((chunk, 4 * width), jnp.bfloat16),
            jax.ShapeDtypeStruct((4, chunk, width), jnp.bfloat16),
            jax.ShapeDtypeStruct((4 * chunk, 2 * width), jnp.bfloat16),
            jax.ShapeDtypeStruct((1, 1), jnp.int32),
        ),
        in_specs=[hbm, hbm, vmem, vmem, smem, smem],
        out_specs=(hbm, hbm, hbm, vmem),
        scratch_shapes=[
            pltpu.VMEM((4, chunk, depth), jnp.bfloat16),
            pltpu.VMEM((3, depth, width), jnp.bfloat16),
            pltpu.VMEM((4, chunk, width), jnp.bfloat16),
            pltpu.VMEM((3, 8 * chunk, 2 * width), jnp.bfloat16),
            pltpu.VMEM((4, heads, chunk, 2 * HD), jnp.float32),
            pltpu.VMEM((4, chunk, width), jnp.bfloat16),
            pltpu.VMEM((2, chunk // 2, width), jnp.bfloat16),
            pltpu.VMEM((n_dp, 8, 128), jnp.int32),
            pltpu.SMEM((24,), jnp.float32),
            dma,
            dma((3,)),
            dma((8,)),
            dma((8,)),
            dma((5, 5)),
            dma((5, 5)),
            dma((6,)),
            dma((6,)),
            dma((n_dp - 1,)),
            dma((n_dp - 1,)),
            dma((6,)),
        ],
        compiler_params=pltpu.CompilerParams(
            collective_id=0, has_side_effects=True, vmem_limit_bytes=60 * 1024 * 1024
        ),
    )(hidden, weight, bias, gains, lists, counts)


def any_lists(query, key_value, tile_lists, tile_counts):
    n_blk = lax.axis_size("blk")
    place = lax.axis_index("blk")
    h = lax.axis_index("head")
    chunk, width = query.shape[1:]
    heads = width // HD
    rows = 2 * TILE
    half, quarter = chunk // 2, chunk // 4

    def in_order(own, right, opposite, left):
        around = jnp.concatenate([own, right, opposite, left] * 2, axis=0)
        return lax.dynamic_slice_in_dim(around, lax.rem(4 - h, 4) * chunk, rows, 0)

    odd = lax.rem(h, 2) == 1
    right_q = jnp.where(odd, query[2], query[1])
    left_q = jnp.where(odd, query[1], query[2])
    query = in_order(query[0], right_q, query[3], left_q).reshape(rows, heads, HD)
    one, two, opp = (key_value[i * chunk : (i + 1) * chunk] for i in (1, 2, 3))
    current = in_order(
        key_value[:chunk],
        jnp.concatenate([two[half:], one[half:]], axis=0),
        jnp.concatenate([opp[:quarter], opp[half:], opp[quarter:half]], axis=0),
        jnp.concatenate([one[:half], two[:half]], axis=0),
    )
    lists = lax.dynamic_slice_in_dim(tile_lists, place * 2, 2, 0)
    counts = lax.dynamic_slice_in_dim(tile_counts, place * 2, 2, 0)
    live = jnp.arange(lists.shape[1], dtype=jnp.int32)[None, :] < counts[:, None]
    route = [(i, (i - 1) % n_blk) for i in range(n_blk)]

    def turn(step, carry):
        total, numer, block = carry
        key_tile = 2 * ((place + step) % n_blk) + jnp.arange(rows, dtype=jnp.int32) // TILE
        hits = (lists[:, :, None] == key_tile[None, None, :]) & live[:, :, None]
        mask = jnp.repeat(jnp.any(hits, axis=1), TILE, axis=0)
        keys = block[:, :width].reshape(rows, heads, HD)
        values = block[:, width:].reshape(rows, heads, HD)
        score = jnp.einsum("qhd,khd->hqk", query, keys, preferred_element_type=jnp.float32)
        w = jnp.where(mask[None], jnp.exp(score * HD ** (-0.5)), jnp.float32(0.0))
        total = total + jnp.sum(w, axis=-1)
        numer = numer + jnp.einsum(
            "hqk,khd->hqd", w.astype(jnp.bfloat16), values, preferred_element_type=jnp.float32
        )
        return (total, numer, lax.ppermute(block, "blk", route))

    total, numer, current = lax.fori_loop(
        0,
        n_blk,
        turn,
        (
            jnp.zeros((heads, rows), jnp.float32),
            jnp.zeros((heads, rows, HD), jnp.float32),
            current,
        ),
    )
    attended = (numer / total[:, :, None]).transpose(1, 0, 2).reshape(rows, width)
    return lax.all_to_all(
        attended.astype(jnp.bfloat16), "head", split_axis=0, concat_axis=1, tiled=True
    )


def shards(hidden, qkv_weight, qkv_bias, norm_gains, tile_lists, tile_counts):
    out, query, key_value, flag = window_attention(
        hidden, qkv_weight, qkv_bias, norm_gains, tile_lists.T, tile_counts
    )
    return lax.cond(
        flag[0, 0] > 0,
        lambda: any_lists(query, key_value, tile_lists, tile_counts),
        lambda: out,
    )


def solution(mesh):
    return jax.shard_map(
        shards,
        mesh=mesh,
        in_specs=(
            P(("dp", "blk", "head"), None),
            P(None, None, "head"),
            P(None, "head"),
            P(),
            P("dp", None),
            P("dp"),
        ),
        out_specs=P(("dp", "blk", "head"), None),
        check_vma=False,
    )
```

```python
import functools

import jax
import jax.numpy as jnp
from jax import lax
from jax.experimental import pallas as pl
from jax.experimental.pallas import tpu as pltpu
from jax.sharding import PartitionSpec as P

HD = 128
TILE = 384
MESH = pl.DeviceIdType.MESH


def kernel(
    sizes,
    hidden, weight, bias, gains, lists, counts,
    out, q_out, kv_out, flag_out,
    hid, wv, qb, kv, acc, ob, passing, flags, mask,
    own_sem, w_sem, hs_sem, hr_sem, ks_sem, kr_sem, os_sem, or_sem, fs_sem, fr_sem, x_sem,
):
    n_blk, n_dp, heads, slots, n_tiles = sizes
    chunk = hid.shape[1]
    half = chunk // 2
    part = chunk // 3
    rest = half - part
    width = heads * HD
    b = lax.axis_index("blk")
    h = lax.axis_index("head")
    d = lax.axis_index("dp")
    c = lax.rem(b, 2)
    z = lax.div(b, 2)
    n_z = n_blk // 2
    right = lax.rem(h + 1, 4)
    opp = lax.rem(h + 2, 4)
    left = lax.rem(h + 3, 4)
    hb = lax.rem(h, 2)
    t0 = lax.div(h, 2)
    mate = h + 1 - 2 * hb
    other = lax.rem(h + 3 + 2 * hb, 4)
    partner = b + 1 - 2 * c
    up = lax.rem(b + 2, n_blk)
    down = lax.rem(b + n_blk - 2, n_blk)
    dps = [lax.rem(d + i, n_dp) for i in range(1, n_dp)]

    own_in = pltpu.make_async_copy(hidden, hid.at[0], own_sem)
    own_in.start()
    w_in = [pltpu.make_async_copy(weight.at[j], wv.at[j], w_sem.at[j]) for j in (1, 2, 0)]
    for copy in w_in:
        copy.start()

    barrier = pltpu.get_barrier_semaphore()
    for p in (right, opp, left):
        pl.semaphore_signal(barrier, inc=1, device_id={"head": p}, device_id_type=MESH)
    for p in (partner, up, down):
        pl.semaphore_signal(barrier, inc=1, device_id={"blk": p}, device_id_type=MESH)
    for p in dps:
        pl.semaphore_signal(barrier, inc=1, device_id={"dp": p}, device_id_type=MESH)
    pl.semaphore_wait(barrier, 6 + len(dps))

    def hid_send(src, slot, start, rows, to, k):
        return pltpu.make_async_remote_copy(
            src_ref=src.at[pl.ds(start, rows)],
            dst_ref=hid.at[slot, pl.ds(start, rows)],
            send_sem=hs_sem.at[k],
            recv_sem=hr_sem.at[k],
            device_id={"head": to},
            device_id_type=MESH,
        )

    hops = [
        hid_send(hidden, 1, 0, half, right, 0),
        hid_send(hidden, 2, half, half, left, 4),
        hid_send(hidden, 1, half, half, right, 1),
        hid_send(hidden, 2, 0, half, left, 5),
        hid_send(hid.at[1], 3, 0, part, right, 2),
        hid_send(hid.at[2], 3, chunk - part, part, left, 6),
        hid_send(hid.at[1], 3, part, rest, right, 3),
        hid_send(hid.at[2], 3, half, rest, left, 7),
    ]
    for copy in hops[:4]:
        copy.start()

    def hid_wait(slot, start, rows, k):
        ref = hid.at[slot, pl.ds(start, rows)]
        pltpu.make_async_copy(ref, ref, hr_sem.at[k]).wait()

    mate_left = hb
    left_block = 2 - mate_left
    right_block = 1 + mate_left
    batches = [
        (0, chunk, [(0, 0, chunk, 0, 0)]),
        (2 * chunk, chunk, [(1, 0, half, left_block, 0), (2, half, half, right_block, half)]),
        (4 * chunk, chunk, [(1, half, half, left_block, half), (2, 0, half, right_block, 0)]),
        (6 * chunk, 2 * part, [(3, 0, part, 3, 0), (3, chunk - part, part, 3, chunk - part)]),
        (6 * chunk + 4 * part, 2 * rest, [(3, part, 2 * rest, 3, part)]),
    ]

    def key_rows(n, core):
        first, rows, _ = batches[n]
        return pl.ds(pl.multiple_of(first + core * rows, rows), rows)

    def kv_copy(src_f, dst_f, n, to, kind):
        rows = key_rows(n, c)
        return pltpu.make_async_remote_copy(
            src_ref=kv.at[src_f, rows],
            dst_ref=kv.at[dst_f, rows],
            send_sem=ks_sem.at[kind, n],
            recv_sem=kr_sem.at[kind, n],
            device_id={"blk": to},
            device_id_type=MESH,
        )

    def kv_wait(f, n, core, kind):
        ref = kv.at[f, key_rows(n, core)]
        pltpu.make_async_copy(ref, ref, kr_sem.at[kind, n]).wait()

    def project(n):
        _, _, pieces = batches[n]
        parts = [hid[slot, start : start + rows] for slot, start, rows, _, _ in pieces]
        x = parts[0] if len(parts) == 1 else jnp.concatenate(parts, axis=0)
        def normed(piece, j):
            mean_sq = jnp.mean(piece * piece, axis=-1, keepdims=True)
            return piece * lax.rsqrt(mean_sq + 1e-06) * gains[j : j + 1, :]

        def bias_of(j):
            return bias[j : j + 1, :].astype(jnp.float32)

        if n == 0:
            w_in[0].wait()
            w_in[1].wait()
        both = jnp.concatenate([wv[1], wv[2]], axis=1)
        made = jnp.dot(x, both, preferred_element_type=jnp.float32)
        made = made + jnp.concatenate([bias_of(1), bias_of(2)], axis=1)
        for g in range(2 * heads):
            piece = made[:, g * HD : (g + 1) * HD]
            if g < heads:
                piece = normed(piece, 1)
            kv[1, key_rows(n, c), g * HD : (g + 1) * HD] = piece.astype(jnp.bfloat16)
        kv_copy(1, 2, n, down, 2).start()
        kv_copy(1, 0, n, up, 1).start()
        kv_copy(1, 1, n, partner, 0).start()
        if n == 0:
            w_in[2].wait()
        made = jnp.dot(x, wv[0], preferred_element_type=jnp.float32) + bias_of(0)
        for g in range(heads):
            cols = slice(g * HD, (g + 1) * HD)
            piece = normed(made[:, cols], 0).astype(jnp.bfloat16)
            at = 0
            for _, _, rows, block, start in pieces:
                qb[block, start : start + rows, cols] = piece[at : at + rows]
                at += rows

    def relay(n):
        kv_wait(0, n, c, 1)
        kv_copy(0, 0, n, partner, 3).start()
        kv_wait(2, n, c, 2)
        kv_copy(2, 2, n, partner, 4).start()

    def near(n):
        kv_wait(1, n, 1 - c, 0)

    def far(n):
        kv_wait(0, n, 1 - c, 3)
        kv_wait(2, n, 1 - c, 4)

    own_in.wait()
    project(0)

    def check_row(t, bad):
        n = counts[t]
        for s in range(slots):
            gap = lax.rem(lists[s, t] // 4 - t // 4 + n_z, n_z)
            far_one = jnp.where((gap > 1) & (gap < n_z - 1) & (s < n), 1, 0)
            bad = jnp.maximum(bad, far_one)
        return bad

    bad = lax.fori_loop(0, n_tiles, check_row, jnp.int32(0))
    flags[d] = jnp.full(flags.shape[1:], bad, jnp.int32)

    def mask_entry(i, carry):
        q = i // 12
        f = lax.rem(i // 4, 3)
        kt = lax.rem(i // 2, 2)
        core = lax.rem(i, 2)
        row = 2 * b + lax.rem(t0 + q, 2)
        tile = 4 * lax.rem(z + f + n_z - 1, n_z) + 2 * core + lax.rem(t0 + kt, 2)
        n = counts[row]
        hit = jnp.int32(0)
        for s in range(slots):
            hit = jnp.maximum(hit, jnp.where((lists[s, row] == tile) & (s < n), 1, 0))
        mask[i] = hit.astype(jnp.float32)
        return carry

    lax.fori_loop(0, 24, mask_entry, 0)

    def flag_send(i, to):
        return pltpu.make_async_remote_copy(
            src_ref=flags.at[d],
            dst_ref=flags.at[d],
            send_sem=fs_sem.at[i],
            recv_sem=fr_sem.at[i],
            device_id={"dp": to},
            device_id_type=MESH,
        )

    flag_sends = [flag_send(i, p) for i, p in enumerate(dps)]
    for copy in flag_sends:
        copy.start()

    acc[...] = jnp.zeros_like(acc)

    mixed = [(half, 1 - mate_left), (half, mate_left)]
    segments = [[(chunk, 0)], mixed, mixed, [(2 * part, 1)], [(2 * rest, 1)]]

    def attend(block, count, tile, groups):
        spans = []
        for f, group in groups:
            base = tile * 12 + f * 4
            live = jnp.concatenate(
                [
                    jnp.full((rows, HD), mask[base + kt * 2 + core], jnp.float32)
                    for n in group
                    for core in range(2)
                    for rows, kt in segments[n]
                ],
                axis=0,
            ).astype(jnp.bfloat16)
            first = batches[group[0]][0]
            spans.append((f, slice(first, first + live.shape[0]), live))
        rows = pl.ds(block, count)
        for g in range(heads):
            qh = qb[rows, :, g * HD : (g + 1) * HD].reshape(count * chunk, HD)
            added = None
            for f, keys, live in spans:
                kh = kv[f, keys, g * HD : (g + 1) * HD]
                vh = kv[f, keys, width + g * HD : width + (g + 1) * HD]
                score = lax.dot_general(
                    qh, kh, (((1,), (1,)), ((), ())), preferred_element_type=jnp.float32
                )
                w = jnp.exp(score * HD ** (-0.5)).astype(jnp.bfloat16)
                ext = jnp.concatenate([vh * live, live], axis=1)
                term = jnp.dot(w, ext, preferred_element_type=jnp.float32)
                added = term if added is None else added + term
            acc[rows, g] += added.reshape(count, chunk, 2 * HD)

    def finish(block):
        for g in range(heads):
            full = acc[block, g]
            ob[block, :, g * HD : (g + 1) * HD] = (full[:, :HD] / full[:, HD:]).astype(jnp.bfloat16)

    def columns(p):
        return pl.ds(pl.multiple_of(p * width, width), width)

    def out_send(src, dst, to, k):
        return pltpu.make_async_remote_copy(
            src_ref=src,
            dst_ref=dst,
            send_sem=os_sem.at[k],
            recv_sem=or_sem.at[k],
            device_id={"head": to},
            device_id_type=MESH,
        )

    upper, lower = pl.ds(0, half), pl.ds(half, half)
    out_sends = [
        out_send(ob.at[3, upper], passing.at[0], right, 0),
        out_send(ob.at[3, lower], passing.at[1], left, 1),
        out_send(ob.at[2], out.at[:, columns(h)], other, 2),
        out_send(ob.at[1], out.at[:, columns(h)], mate, 3),
        out_send(passing.at[0], out.at[upper, columns(left)], right, 4),
        out_send(passing.at[1], out.at[lower, columns(right)], left, 5),
    ]
    own_out = pltpu.make_async_copy(ob.at[0], out.at[:, columns(h)], own_sem)

    hid_wait(1, 0, half, 0)
    hops[4].start()
    hops[6].start()
    hid_wait(2, half, half, 4)
    hops[5].start()
    hops[7].start()
    relay(0)
    project(1)
    for i in range(n_dp - 1):
        src = lax.rem(d + n_dp - 1 - i, n_dp)
        ref = flags.at[src]
        pltpu.make_async_copy(ref, ref, fr_sem.at[i]).wait()
    flag_out[...] = jnp.max(flags[:, 0:1, 0:1], axis=0)
    near(0)
    near(1)

    def own_first(i, carry):
        @pl.when(i == 1)
        def _():
            relay(1)
            far(0)
            far(1)

        attend(0, 1, 0, [(lax.rem(2 * i + 1, 3), (0, 1))])
        return carry

    lax.fori_loop(0, 3, own_first, 0)
    hid_wait(1, half, half, 1)
    hid_wait(2, 0, half, 5)
    project(2)

    def neighbours_first(i, carry):
        attend(1 + i, 1, i, [(f, (0, 1)) for f in range(3)])
        return carry

    lax.fori_loop(0, 2, neighbours_first, 0)
    hid_wait(3, 0, part, 2)
    hid_wait(3, chunk - part, part, 6)
    project(3)
    relay(2)
    near(2)
    near(3)
    attend(0, 2, 0, [(1, (2, 3))])
    hid_wait(3, part, rest, 3)
    hid_wait(3, half, rest, 7)
    project(4)
    attend(3, 1, 1, [(f, (0, 1)) for f in range(3)])
    keep = [pltpu.make_async_copy(qb, q_out, x_sem.at[5])]
    at = 0
    for n, (_, rows, _) in enumerate(batches):
        keep.append(pltpu.make_async_copy(kv.at[1, key_rows(n, c)], kv_out.at[pl.ds(at, rows)], x_sem.at[n]))
        at += rows
    for copy in keep:
        copy.start()
    relay(3)
    attend(2, 2, 1, [(1, (2, 3))])
    far(2)
    far(3)

    def second(i, carry):
        @pl.when(i == 1)
        def _():
            relay(4)

        attend(2 - 2 * i, 2, 1 - i, [(0, (2, 3)), (2, (2, 3))])
        return carry

    lax.fori_loop(0, 2, second, 0)
    near(4)
    far(4)

    def last(i, carry):
        attend(2 - 2 * i, 2, 1 - i, [(f, (4,)) for f in range(3)])
        finish(3 - 2 * i)

        @pl.when(i == 0)
        def _():
            out_sends[0].start()
            out_sends[1].start()

        finish(2 - 2 * i)

        @pl.when(i == 0)
        def _():
            out_sends[2].start()

        @pl.when(i == 1)
        def _():
            out_sends[3].start()

        return carry

    lax.fori_loop(0, 2, last, 0)
    own_out.start()
    for k in range(2):
        ref = passing.at[k]
        pltpu.make_async_copy(ref, ref, or_sem.at[k]).wait()
        out_sends[4 + k].start()

    for copy in hops:
        copy.wait_send()
    for n in range(5):
        kv_copy(1, 1, n, partner, 0).wait_send()
        kv_copy(1, 0, n, up, 1).wait_send()
        kv_copy(1, 2, n, down, 2).wait_send()
        kv_copy(0, 0, n, partner, 3).wait_send()
        kv_copy(2, 2, n, partner, 4).wait_send()
    for copy in flag_sends:
        copy.wait_send()
    for copy in keep:
        copy.wait()
    own_out.wait()
    for copy in out_sends:
        copy.wait_send()
    for k, ref in (
        (2, out.at[:, columns(other)]),
        (3, out.at[:, columns(mate)]),
        (4, out.at[upper, columns(opp)]),
        (5, out.at[lower, columns(opp)]),
    ):
        pltpu.make_async_copy(ref, ref, or_sem.at[k]).wait()


def window_attention(hidden, weight, bias, gains, lists, counts):
    n_blk = lax.axis_size("blk")
    n_dp = lax.axis_size("dp")
    chunk, depth = hidden.shape
    width = weight.shape[2]
    heads = width // HD
    slots, n_tiles = lists.shape
    sizes = (n_blk, n_dp, heads, slots, n_tiles)
    hbm = pl.BlockSpec(memory_space=pl.ANY)
    vmem = pl.BlockSpec(memory_space=pltpu.VMEM)
    smem = pl.BlockSpec(memory_space=pltpu.SMEM)
    dma = pltpu.SemaphoreType.DMA
    return pl.pallas_call(
        functools.partial(kernel, sizes),
        out_shape=(
            jax.ShapeDtypeStruct((chunk, 4 * width), jnp.bfloat16),
            jax.ShapeDtypeStruct((4, chunk, width), jnp.bfloat16),
            jax.ShapeDtypeStruct((4 * chunk, 2 * width), jnp.bfloat16),
            jax.ShapeDtypeStruct((1, 1), jnp.int32),
        ),
        in_specs=[hbm, hbm, vmem, vmem, smem, smem],
        out_specs=(hbm, hbm, hbm, vmem),
        scratch_shapes=[
            pltpu.VMEM((4, chunk, depth), jnp.bfloat16),
            pltpu.VMEM((3, depth, width), jnp.bfloat16),
            pltpu.VMEM((4, chunk, width), jnp.bfloat16),
            pltpu.VMEM((3, 8 * chunk, 2 * width), jnp.bfloat16),
            pltpu.VMEM((4, heads, chunk, 2 * HD), jnp.float32),
            pltpu.VMEM((4, chunk, width), jnp.bfloat16),
            pltpu.VMEM((2, chunk // 2, width), jnp.bfloat16),
            pltpu.VMEM((n_dp, 8, 128), jnp.int32),
            pltpu.SMEM((24,), jnp.float32),
            dma,
            dma((3,)),
            dma((8,)),
            dma((8,)),
            dma((5, 5)),
            dma((5, 5)),
            dma((6,)),
            dma((6,)),
            dma((n_dp - 1,)),
            dma((n_dp - 1,)),
            dma((6,)),
        ],
        compiler_params=pltpu.CompilerParams(
            collective_id=0, has_side_effects=True, vmem_limit_bytes=60 * 1024 * 1024
        ),
    )(hidden, weight, bias, gains, lists, counts)


def any_lists(query, key_value, tile_lists, tile_counts):
    n_blk = lax.axis_size("blk")
    place = lax.axis_index("blk")
    h = lax.axis_index("head")
    chunk, width = query.shape[1:]
    heads = width // HD
    rows = 2 * TILE
    half, part = chunk // 2, chunk // 3

    def in_order(own, right, opposite, left):
        around = jnp.concatenate([own, right, opposite, left] * 2, axis=0)
        return lax.dynamic_slice_in_dim(around, lax.rem(4 - h, 4) * chunk, rows, 0)

    odd = lax.rem(h, 2) == 1
    right_q = jnp.where(odd, query[2], query[1])
    left_q = jnp.where(odd, query[1], query[2])
    query = in_order(query[0], right_q, query[3], left_q).reshape(rows, heads, HD)
    one, two, opp = (key_value[i * chunk : (i + 1) * chunk] for i in (1, 2, 3))
    current = in_order(
        key_value[:chunk],
        jnp.concatenate([two[half:], one[half:]], axis=0),
        jnp.concatenate([opp[:part], opp[2 * part :], opp[part : 2 * part]], axis=0),
        jnp.concatenate([one[:half], two[:half]], axis=0),
    )
    lists = lax.dynamic_slice_in_dim(tile_lists, place * 2, 2, 0)
    counts = lax.dynamic_slice_in_dim(tile_counts, place * 2, 2, 0)
    live = jnp.arange(lists.shape[1], dtype=jnp.int32)[None, :] < counts[:, None]
    route = [(i, (i - 1) % n_blk) for i in range(n_blk)]

    def turn(step, carry):
        total, numer, block = carry
        key_tile = 2 * ((place + step) % n_blk) + jnp.arange(rows, dtype=jnp.int32) // TILE
        hits = (lists[:, :, None] == key_tile[None, None, :]) & live[:, :, None]
        mask = jnp.repeat(jnp.any(hits, axis=1), TILE, axis=0)
        keys = block[:, :width].reshape(rows, heads, HD)
        values = block[:, width:].reshape(rows, heads, HD)
        score = jnp.einsum("qhd,khd->hqk", query, keys, preferred_element_type=jnp.float32)
        w = jnp.where(mask[None], jnp.exp(score * HD ** (-0.5)), jnp.float32(0.0))
        total = total + jnp.sum(w, axis=-1)
        numer = numer + jnp.einsum(
            "hqk,khd->hqd", w.astype(jnp.bfloat16), values, preferred_element_type=jnp.float32
        )
        return (total, numer, lax.ppermute(block, "blk", route))

    total, numer, current = lax.fori_loop(
        0,
        n_blk,
        turn,
        (
            jnp.zeros((heads, rows), jnp.float32),
            jnp.zeros((heads, rows, HD), jnp.float32),
            current,
        ),
    )
    attended = (numer / total[:, :, None]).transpose(1, 0, 2).reshape(rows, width)
    return lax.all_to_all(
        attended.astype(jnp.bfloat16), "head", split_axis=0, concat_axis=1, tiled=True
    )


def shards(hidden, qkv_weight, qkv_bias, norm_gains, tile_lists, tile_counts):
    out, query, key_value, flag = window_attention(
        hidden, qkv_weight, qkv_bias, norm_gains, tile_lists.T, tile_counts
    )
    return lax.cond(
        flag[0, 0] > 0,
        lambda: any_lists(query, key_value, tile_lists, tile_counts),
        lambda: out,
    )


def solution(mesh):
    return jax.shard_map(
        shards,
        mesh=mesh,
        in_specs=(
            P(("dp", "blk", "head"), None),
            P(None, None, "head"),
            P(None, "head"),
            P(),
            P("dp", None),
            P("dp"),
        ),
        out_specs=P(("dp", "blk", "head"), None),
        check_vma=False,
    )
```

```python
import functools

import jax
import jax.numpy as jnp
from jax import lax
from jax.experimental import pallas as pl
from jax.experimental.pallas import tpu as pltpu
from jax.sharding import PartitionSpec as P

HD = 128
TILE = 384
MESH = pl.DeviceIdType.MESH


def kernel(
    sizes,
    hidden, weight, bias_in, gains_in, lists_in, counts_in,
    out, q_out, kv_out, flag_out,
    hid, wv, qb, kv, acc, ob, passing, flags, mask,
    bias, gains, lists, counts,
    own_sem, w_sem, hs_sem, hr_sem, ks_sem, kr_sem, os_sem, or_sem, fs_sem, fr_sem, x_sem, s_sem,
):
    n_blk, n_dp, heads, slots, n_tiles = sizes
    chunk = hid.shape[1]
    half = chunk // 2
    part = chunk // 3
    rest = half - part
    width = heads * HD
    b = lax.axis_index("blk")
    h = lax.axis_index("head")
    d = lax.axis_index("dp")
    c = lax.rem(b, 2)
    z = lax.div(b, 2)
    n_z = n_blk // 2
    right = lax.rem(h + 1, 4)
    opp = lax.rem(h + 2, 4)
    left = lax.rem(h + 3, 4)
    hb = lax.rem(h, 2)
    t0 = lax.div(h, 2)
    mate = h + 1 - 2 * hb
    other = lax.rem(h + 3 + 2 * hb, 4)
    partner = b + 1 - 2 * c
    up = lax.rem(b + 2, n_blk)
    down = lax.rem(b + n_blk - 2, n_blk)
    d_up = lax.rem(d + 1, n_dp)
    d_down = lax.rem(d + n_dp - 1, n_dp)

    barrier = pltpu.get_barrier_semaphore()
    for p in (right, left):
        pl.semaphore_signal(barrier, inc=1, device_id={"head": p}, device_id_type=MESH)
    for p in (up, down, partner):
        pl.semaphore_signal(barrier, inc=1, device_id={"blk": p}, device_id_type=MESH)
    for p in (d_up, d_down):
        pl.semaphore_signal(barrier, inc=1, device_id={"dp": p}, device_id_type=MESH)
    own_in = pltpu.make_async_copy(hidden, hid.at[0], own_sem)
    own_in.start()
    w_in = [pltpu.make_async_copy(weight.at[j], wv.at[j], w_sem.at[j]) for j in (1, 2, 0)]
    for copy in w_in:
        copy.start()
    small = [
        pltpu.make_async_copy(src, dst, s_sem.at[k])
        for k, (src, dst) in enumerate(
            ((bias_in, bias), (gains_in, gains), (lists_in, lists), (counts_in, counts))
        )
    ]
    for copy in small:
        copy.start()
    pl.semaphore_wait(barrier, 7)

    def hid_send(src, slot, start, rows, to, k):
        return pltpu.make_async_remote_copy(
            src_ref=src.at[pl.ds(start, rows)],
            dst_ref=hid.at[slot, pl.ds(start, rows)],
            send_sem=hs_sem.at[k],
            recv_sem=hr_sem.at[k],
            device_id={"head": to},
            device_id_type=MESH,
        )

    hops = [
        hid_send(hidden, 1, 0, half, right, 0),
        hid_send(hidden, 2, half, half, left, 4),
        hid_send(hidden, 1, half, half, right, 1),
        hid_send(hidden, 2, 0, half, left, 5),
        hid_send(hid.at[1], 3, 0, part, right, 2),
        hid_send(hid.at[2], 3, chunk - part, part, left, 6),
        hid_send(hid.at[1], 3, part, rest, right, 3),
        hid_send(hid.at[2], 3, half, rest, left, 7),
    ]
    for copy in hops[:4]:
        copy.start()

    def hid_wait(slot, start, rows, k):
        ref = hid.at[slot, pl.ds(start, rows)]
        pltpu.make_async_copy(ref, ref, hr_sem.at[k]).wait()

    mate_left = hb
    left_block = 2 - mate_left
    right_block = 1 + mate_left
    batches = [
        (0, chunk, [(0, 0, chunk, 0, 0)]),
        (2 * chunk, chunk, [(1, 0, half, left_block, 0), (2, half, half, right_block, half)]),
        (4 * chunk, chunk, [(1, half, half, left_block, half), (2, 0, half, right_block, 0)]),
        (6 * chunk, 2 * part, [(3, 0, part, 3, 0), (3, chunk - part, part, 3, chunk - part)]),
        (6 * chunk + 4 * part, 2 * rest, [(3, part, 2 * rest, 3, part)]),
    ]

    def key_rows(n, core):
        first, rows, _ = batches[n]
        return pl.ds(pl.multiple_of(first + core * rows, rows), rows)

    def kv_copy(src_f, dst_f, n, to, kind):
        rows = key_rows(n, c)
        return pltpu.make_async_remote_copy(
            src_ref=kv.at[src_f, rows],
            dst_ref=kv.at[dst_f, rows],
            send_sem=ks_sem.at[kind, n],
            recv_sem=kr_sem.at[kind, n],
            device_id={"blk": to},
            device_id_type=MESH,
        )

    def kv_wait(f, n, core, kind):
        ref = kv.at[f, key_rows(n, core)]
        pltpu.make_async_copy(ref, ref, kr_sem.at[kind, n]).wait()

    def project(n):
        _, _, pieces = batches[n]
        parts = [hid[slot, start : start + rows] for slot, start, rows, _, _ in pieces]
        x = parts[0] if len(parts) == 1 else jnp.concatenate(parts, axis=0)
        def normed(piece, j):
            mean_sq = jnp.mean(piece * piece, axis=-1, keepdims=True)
            return piece * lax.rsqrt(mean_sq + 1e-06) * gains[j : j + 1, :]

        def bias_of(j):
            return bias[j : j + 1, :].astype(jnp.float32)

        if n == 0:
            w_in[0].wait()
            w_in[1].wait()
        both = jnp.concatenate([wv[1], wv[2]], axis=1)
        made = jnp.dot(x, both, preferred_element_type=jnp.float32)
        made = made + jnp.concatenate([bias_of(1), bias_of(2)], axis=1)
        for g in range(2 * heads):
            piece = made[:, g * HD : (g + 1) * HD]
            if g < heads:
                piece = normed(piece, 1)
            kv[1, key_rows(n, c), g * HD : (g + 1) * HD] = piece.astype(jnp.bfloat16)
        kv_copy(1, 2, n, down, 2).start()
        kv_copy(1, 0, n, up, 1).start()
        kv_copy(1, 1, n, partner, 0).start()
        if n == 0:
            w_in[2].wait()
        made = jnp.dot(x, wv[0], preferred_element_type=jnp.float32) + bias_of(0)
        for g in range(heads):
            cols = slice(g * HD, (g + 1) * HD)
            piece = normed(made[:, cols], 0).astype(jnp.bfloat16)
            at = 0
            for _, _, rows, block, start in pieces:
                qb[block, start : start + rows, cols] = piece[at : at + rows]
                at += rows

    def relay(n):
        kv_wait(0, n, c, 1)
        kv_copy(0, 0, n, partner, 3).start()
        kv_wait(2, n, c, 2)
        kv_copy(2, 2, n, partner, 4).start()

    def near(n):
        kv_wait(1, n, 1 - c, 0)

    def far(n):
        kv_wait(0, n, 1 - c, 3)
        kv_wait(2, n, 1 - c, 4)

    own_in.wait()
    small[0].wait()
    small[1].wait()
    project(0)
    small[2].wait()
    small[3].wait()

    def check_row(t, bad):
        n = counts[t]
        for s in range(slots):
            gap = lax.rem(lists[s, t] // 4 - t // 4 + n_z, n_z)
            far_one = jnp.where((gap > 1) & (gap < n_z - 1) & (s < n), 1, 0)
            bad = jnp.maximum(bad, far_one)
        return bad

    bad = lax.fori_loop(0, n_tiles, check_row, jnp.int32(0))
    flags[0] = jnp.full(flags.shape[1:], bad, jnp.int32)

    def mask_entry(i, carry):
        q = i // 12
        f = lax.rem(i // 4, 3)
        kt = lax.rem(i // 2, 2)
        core = lax.rem(i, 2)
        row = 2 * b + lax.rem(t0 + q, 2)
        tile = 4 * lax.rem(z + f + n_z - 1, n_z) + 2 * core + lax.rem(t0 + kt, 2)
        n = counts[row]
        hit = jnp.int32(0)
        for s in range(slots):
            hit = jnp.maximum(hit, jnp.where((lists[s, row] == tile) & (s < n), 1, 0))
        mask[i] = hit.astype(jnp.float32)
        return carry

    lax.fori_loop(0, 24, mask_entry, 0)

    def flag_send(src, dst, to, k):
        return pltpu.make_async_remote_copy(
            src_ref=flags.at[src],
            dst_ref=flags.at[dst],
            send_sem=fs_sem.at[k],
            recv_sem=fr_sem.at[k],
            device_id={"dp": to},
            device_id_type=MESH,
        )

    flag_sends = [flag_send(0, 1, d_up, 0), flag_send(0, 2, d_down, 1), flag_send(3, 4, d_up, 2)]
    flag_sends[0].start()
    flag_sends[1].start()

    def flag_wait(dst, k):
        ref = flags.at[dst]
        pltpu.make_async_copy(ref, ref, fr_sem.at[k]).wait()

    acc[...] = jnp.zeros_like(acc)

    mixed = [(half, 1 - mate_left), (half, mate_left)]
    segments = [[(chunk, 0)], mixed, mixed, [(2 * part, 1)], [(2 * rest, 1)]]

    def attend(block, count, tile, groups):
        spans = []
        for f, group in groups:
            base = tile * 12 + f * 4
            live = jnp.concatenate(
                [
                    jnp.full((rows, HD), mask[base + kt * 2 + core], jnp.float32)
                    for n in group
                    for core in range(2)
                    for rows, kt in segments[n]
                ],
                axis=0,
            ).astype(jnp.bfloat16)
            first = batches[group[0]][0]
            spans.append((f, slice(first, first + live.shape[0]), live))
        rows = pl.ds(block, count)
        for g in range(heads):
            qh = qb[rows, :, g * HD : (g + 1) * HD].reshape(count * chunk, HD)
            added = None
            for f, keys, live in spans:
                kh = kv[f, keys, g * HD : (g + 1) * HD]
                vh = kv[f, keys, width + g * HD : width + (g + 1) * HD]
                score = lax.dot_general(
                    qh, kh, (((1,), (1,)), ((), ())), preferred_element_type=jnp.float32
                )
                w = jnp.exp(score * HD ** (-0.5)).astype(jnp.bfloat16)
                ext = jnp.concatenate([vh * live, live], axis=1)
                term = jnp.dot(w, ext, preferred_element_type=jnp.float32)
                added = term if added is None else added + term
            acc[rows, g] += added.reshape(count, chunk, 2 * HD)

    def finish(block):
        for g in range(heads):
            full = acc[block, g]
            ob[block, :, g * HD : (g + 1) * HD] = (full[:, :HD] / full[:, HD:]).astype(jnp.bfloat16)

    def columns(p):
        return pl.ds(pl.multiple_of(p * width, width), width)

    def out_send(src, dst, to, k):
        return pltpu.make_async_remote_copy(
            src_ref=src,
            dst_ref=dst,
            send_sem=os_sem.at[k],
            recv_sem=or_sem.at[k],
            device_id={"head": to},
            device_id_type=MESH,
        )

    upper, lower = pl.ds(0, half), pl.ds(half, half)
    out_sends = [
        out_send(ob.at[3, upper], passing.at[0], right, 0),
        out_send(ob.at[3, lower], passing.at[1], left, 1),
        out_send(ob.at[2], out.at[:, columns(h)], other, 2),
        out_send(ob.at[1], out.at[:, columns(h)], mate, 3),
        out_send(passing.at[0], out.at[upper, columns(left)], right, 4),
        out_send(passing.at[1], out.at[lower, columns(right)], left, 5),
    ]
    own_out = pltpu.make_async_copy(ob.at[0], out.at[:, columns(h)], own_sem)

    hid_wait(1, 0, half, 0)
    hops[4].start()
    hops[6].start()
    hid_wait(2, half, half, 4)
    hops[5].start()
    hops[7].start()
    relay(0)
    project(1)
    flag_wait(1, 0)
    flags[3] = jnp.maximum(flags[0], flags[1])
    flag_sends[2].start()
    near(0)
    near(1)

    def own_first(i, carry):
        @pl.when(i == 1)
        def _():
            relay(1)
            far(0)
            far(1)

        attend(0, 1, 0, [(lax.rem(2 * i + 1, 3), (0, 1))])
        return carry

    lax.fori_loop(0, 3, own_first, 0)
    flag_wait(2, 1)
    flag_wait(4, 2)
    seen = jnp.maximum(jnp.maximum(flags[2], flags[3]), flags[4])
    flag_out[...] = seen[0:1, 0:1]
    hid_wait(1, half, half, 1)
    hid_wait(2, 0, half, 5)
    project(2)

    def neighbours_first(i, carry):
        attend(1 + i, 1, i, [(f, (0, 1)) for f in range(3)])
        return carry

    lax.fori_loop(0, 2, neighbours_first, 0)
    hid_wait(3, 0, part, 2)
    hid_wait(3, chunk - part, part, 6)
    project(3)
    relay(2)
    near(2)
    far(2)
    attend(0, 2, 0, [(f, (2,)) for f in range(3)])
    hid_wait(3, part, rest, 3)
    hid_wait(3, half, rest, 7)
    project(4)
    attend(3, 1, 1, [(f, (0, 1)) for f in range(3)])
    keep = [pltpu.make_async_copy(qb, q_out, x_sem.at[5])]
    at = 0
    for n, (_, rows, _) in enumerate(batches):
        keep.append(pltpu.make_async_copy(kv.at[1, key_rows(n, c)], kv_out.at[pl.ds(at, rows)], x_sem.at[n]))
        at += rows
    for copy in keep:
        copy.start()
    relay(3)
    attend(2, 2, 1, [(f, (2,)) for f in range(3)])
    near(3)
    far(3)
    relay(4)

    def second(i, carry):
        attend(2 - 2 * i, 2, 1 - i, [(f, (3,)) for f in range(3)])
        return carry

    lax.fori_loop(0, 2, second, 0)
    near(4)
    far(4)

    def last(i, carry):
        attend(2 - 2 * i, 2, 1 - i, [(f, (4,)) for f in range(3)])
        finish(3 - 2 * i)

        @pl.when(i == 0)
        def _():
            out_sends[0].start()
            out_sends[1].start()

        finish(2 - 2 * i)

        @pl.when(i == 0)
        def _():
            out_sends[2].start()

        @pl.when(i == 1)
        def _():
            out_sends[3].start()

        return carry

    lax.fori_loop(0, 2, last, 0)
    own_out.start()
    for k in range(2):
        ref = passing.at[k]
        pltpu.make_async_copy(ref, ref, or_sem.at[k]).wait()
        out_sends[4 + k].start()

    for copy in hops:
        copy.wait_send()
    for n in range(5):
        kv_copy(1, 1, n, partner, 0).wait_send()
        kv_copy(1, 0, n, up, 1).wait_send()
        kv_copy(1, 2, n, down, 2).wait_send()
        kv_copy(0, 0, n, partner, 3).wait_send()
        kv_copy(2, 2, n, partner, 4).wait_send()
    for copy in flag_sends:
        copy.wait_send()
    for copy in keep:
        copy.wait()
    own_out.wait()
    for copy in out_sends:
        copy.wait_send()
    for k, ref in (
        (2, out.at[:, columns(other)]),
        (3, out.at[:, columns(mate)]),
        (4, out.at[upper, columns(opp)]),
        (5, out.at[lower, columns(opp)]),
    ):
        pltpu.make_async_copy(ref, ref, or_sem.at[k]).wait()


def window_attention(hidden, weight, bias, gains, lists, counts):
    n_blk = lax.axis_size("blk")
    n_dp = lax.axis_size("dp")
    chunk, depth = hidden.shape
    width = weight.shape[2]
    heads = width // HD
    slots, n_tiles = lists.shape
    sizes = (n_blk, n_dp, heads, slots, n_tiles)
    hbm = pl.BlockSpec(memory_space=pl.ANY)
    vmem = pl.BlockSpec(memory_space=pltpu.VMEM)
    dma = pltpu.SemaphoreType.DMA
    return pl.pallas_call(
        functools.partial(kernel, sizes),
        out_shape=(
            jax.ShapeDtypeStruct((chunk, 4 * width), jnp.bfloat16),
            jax.ShapeDtypeStruct((4, chunk, width), jnp.bfloat16),
            jax.ShapeDtypeStruct((4 * chunk, 2 * width), jnp.bfloat16),
            jax.ShapeDtypeStruct((1, 1), jnp.int32),
        ),
        in_specs=[hbm] * 6,
        out_specs=(hbm, hbm, hbm, vmem),
        scratch_shapes=[
            pltpu.VMEM((4, chunk, depth), jnp.bfloat16),
            pltpu.VMEM((3, depth, width), jnp.bfloat16),
            pltpu.VMEM((4, chunk, width), jnp.bfloat16),
            pltpu.VMEM((3, 8 * chunk, 2 * width), jnp.bfloat16),
            pltpu.VMEM((4, heads, chunk, 2 * HD), jnp.float32),
            pltpu.VMEM((4, chunk, width), jnp.bfloat16),
            pltpu.VMEM((2, chunk // 2, width), jnp.bfloat16),
            pltpu.VMEM((5, 8, 128), jnp.int32),
            pltpu.SMEM((24,), jnp.float32),
            pltpu.VMEM(bias.shape, bias.dtype),
            pltpu.VMEM(gains.shape, gains.dtype),
            pltpu.SMEM(lists.shape, lists.dtype),
            pltpu.SMEM(counts.shape, counts.dtype),
            dma,
            dma((3,)),
            dma((8,)),
            dma((8,)),
            dma((5, 5)),
            dma((5, 5)),
            dma((6,)),
            dma((6,)),
            dma((3,)),
            dma((3,)),
            dma((6,)),
            dma((4,)),
        ],
        compiler_params=pltpu.CompilerParams(
            collective_id=0, has_side_effects=True, vmem_limit_bytes=60 * 1024 * 1024
        ),
    )(hidden, weight, bias, gains, lists, counts)


def any_lists(query, key_value, tile_lists, tile_counts):
    n_blk = lax.axis_size("blk")
    place = lax.axis_index("blk")
    h = lax.axis_index("head")
    chunk, width = query.shape[1:]
    heads = width // HD
    rows = 2 * TILE
    half, part = chunk // 2, chunk // 3

    def in_order(own, right, opposite, left):
        around = jnp.concatenate([own, right, opposite, left] * 2, axis=0)
        return lax.dynamic_slice_in_dim(around, lax.rem(4 - h, 4) * chunk, rows, 0)

    odd = lax.rem(h, 2) == 1
    right_q = jnp.where(odd, query[2], query[1])
    left_q = jnp.where(odd, query[1], query[2])
    query = in_order(query[0], right_q, query[3], left_q).reshape(rows, heads, HD)
    one, two, opp = (key_value[i * chunk : (i + 1) * chunk] for i in (1, 2, 3))
    current = in_order(
        key_value[:chunk],
        jnp.concatenate([two[half:], one[half:]], axis=0),
        jnp.concatenate([opp[:part], opp[2 * part :], opp[part : 2 * part]], axis=0),
        jnp.concatenate([one[:half], two[:half]], axis=0),
    )
    lists = lax.dynamic_slice_in_dim(tile_lists, place * 2, 2, 0)
    counts = lax.dynamic_slice_in_dim(tile_counts, place * 2, 2, 0)
    live = jnp.arange(lists.shape[1], dtype=jnp.int32)[None, :] < counts[:, None]
    route = [(i, (i - 1) % n_blk) for i in range(n_blk)]

    def turn(step, carry):
        total, numer, block = carry
        key_tile = 2 * ((place + step) % n_blk) + jnp.arange(rows, dtype=jnp.int32) // TILE
        hits = (lists[:, :, None] == key_tile[None, None, :]) & live[:, :, None]
        mask = jnp.repeat(jnp.any(hits, axis=1), TILE, axis=0)
        keys = block[:, :width].reshape(rows, heads, HD)
        values = block[:, width:].reshape(rows, heads, HD)
        score = jnp.einsum("qhd,khd->hqk", query, keys, preferred_element_type=jnp.float32)
        w = jnp.where(mask[None], jnp.exp(score * HD ** (-0.5)), jnp.float32(0.0))
        total = total + jnp.sum(w, axis=-1)
        numer = numer + jnp.einsum(
            "hqk,khd->hqd", w.astype(jnp.bfloat16), values, preferred_element_type=jnp.float32
        )
        return (total, numer, lax.ppermute(block, "blk", route))

    total, numer, current = lax.fori_loop(
        0,
        n_blk,
        turn,
        (
            jnp.zeros((heads, rows), jnp.float32),
            jnp.zeros((heads, rows, HD), jnp.float32),
            current,
        ),
    )
    attended = (numer / total[:, :, None]).transpose(1, 0, 2).reshape(rows, width)
    return lax.all_to_all(
        attended.astype(jnp.bfloat16), "head", split_axis=0, concat_axis=1, tiled=True
    )


def shards(hidden, qkv_weight, qkv_bias, norm_gains, tile_lists, tile_counts):
    out, query, key_value, flag = window_attention(
        hidden, qkv_weight, qkv_bias, norm_gains, tile_lists.T, tile_counts
    )
    return lax.cond(
        flag[0, 0] > 0,
        lambda: any_lists(query, key_value, tile_lists, tile_counts),
        lambda: out,
    )


def solution(mesh):
    return jax.shard_map(
        shards,
        mesh=mesh,
        in_specs=(
            P(("dp", "blk", "head"), None),
            P(None, None, "head"),
            P(None, "head"),
            P(),
            P("dp", None),
            P("dp"),
        ),
        out_specs=P(("dp", "blk", "head"), None),
        check_vma=False,
    )
```

```python
import functools

import jax
import jax.numpy as jnp
from jax import lax
from jax.experimental import pallas as pl
from jax.experimental.pallas import tpu as pltpu
from jax.sharding import PartitionSpec as P

HD = 128
TILE = 384
MESH = pl.DeviceIdType.MESH


def kernel(
    sizes,
    hidden, weight, bias_in, gains_in, lists_in, counts_in,
    out, q_out, kv_out, flag_out,
    hid, wv, qb, kv, acc, ob, passing, flags, mask,
    bias, gains, lists, counts,
    own_sem, w_sem, hs_sem, hr_sem, ks_sem, kr_sem, os_sem, or_sem, fs_sem, fr_sem, x_sem, s_sem,
):
    n_blk, n_dp, heads, slots, n_tiles = sizes
    chunk = hid.shape[1]
    half = chunk // 2
    part = chunk // 3
    rest = half - part
    width = heads * HD
    b = lax.axis_index("blk")
    h = lax.axis_index("head")
    d = lax.axis_index("dp")
    c = lax.rem(b, 2)
    z = lax.div(b, 2)
    n_z = n_blk // 2
    right = lax.rem(h + 1, 4)
    opp = lax.rem(h + 2, 4)
    left = lax.rem(h + 3, 4)
    hb = lax.rem(h, 2)
    t0 = lax.div(h, 2)
    mate = h + 1 - 2 * hb
    other = lax.rem(h + 3 + 2 * hb, 4)
    partner = b + 1 - 2 * c
    up = lax.rem(b + 2, n_blk)
    down = lax.rem(b + n_blk - 2, n_blk)
    d_up = lax.rem(d + 1, n_dp)
    d_down = lax.rem(d + n_dp - 1, n_dp)

    barrier = pltpu.get_barrier_semaphore()
    for p in (right, left):
        pl.semaphore_signal(barrier, inc=1, device_id={"head": p}, device_id_type=MESH)
    for p in (up, down, partner):
        pl.semaphore_signal(barrier, inc=1, device_id={"blk": p}, device_id_type=MESH)
    for p in (d_up, d_down):
        pl.semaphore_signal(barrier, inc=1, device_id={"dp": p}, device_id_type=MESH)
    own_in = pltpu.make_async_copy(hidden, hid.at[0], own_sem)
    own_in.start()
    w_in = [pltpu.make_async_copy(weight.at[j], wv.at[j], w_sem.at[j]) for j in (1, 2, 0)]
    for copy in w_in:
        copy.start()
    small = [
        pltpu.make_async_copy(src, dst, s_sem.at[k])
        for k, (src, dst) in enumerate(
            ((bias_in, bias), (gains_in, gains), (lists_in, lists), (counts_in, counts))
        )
    ]
    for copy in small:
        copy.start()
    pl.semaphore_wait(barrier, 7)

    def hid_send(src, slot, start, rows, to, k):
        return pltpu.make_async_remote_copy(
            src_ref=src.at[pl.ds(start, rows)],
            dst_ref=hid.at[slot, pl.ds(start, rows)],
            send_sem=hs_sem.at[k],
            recv_sem=hr_sem.at[k],
            device_id={"head": to},
            device_id_type=MESH,
        )

    hops = [
        hid_send(hidden, 1, 0, half, right, 0),
        hid_send(hidden, 2, half, half, left, 4),
        hid_send(hidden, 1, half, half, right, 1),
        hid_send(hidden, 2, 0, half, left, 5),
        hid_send(hid.at[1], 3, 0, part, right, 2),
        hid_send(hid.at[2], 3, chunk - part, part, left, 6),
        hid_send(hid.at[1], 3, part, rest, right, 3),
        hid_send(hid.at[2], 3, half, rest, left, 7),
    ]
    for copy in hops[:4]:
        copy.start()

    def hid_wait(slot, start, rows, k):
        ref = hid.at[slot, pl.ds(start, rows)]
        pltpu.make_async_copy(ref, ref, hr_sem.at[k]).wait()

    mate_left = hb
    left_block = 2 - mate_left
    right_block = 1 + mate_left
    batches = [
        (0, chunk, [(0, 0, chunk, 0, 0)]),
        (2 * chunk, chunk, [(1, 0, half, left_block, 0), (2, half, half, right_block, half)]),
        (4 * chunk, chunk, [(1, half, half, left_block, half), (2, 0, half, right_block, 0)]),
        (6 * chunk, 2 * part, [(3, 0, part, 3, 0), (3, chunk - part, part, 3, chunk - part)]),
        (6 * chunk + 4 * part, 2 * rest, [(3, part, 2 * rest, 3, part)]),
    ]

    def key_rows(n, core):
        first, rows, _ = batches[n]
        return pl.ds(pl.multiple_of(first + core * rows, rows), rows)

    def kv_copy(src_f, dst_f, n, to, kind):
        rows = key_rows(n, c)
        return pltpu.make_async_remote_copy(
            src_ref=kv.at[src_f, rows],
            dst_ref=kv.at[dst_f, rows],
            send_sem=ks_sem.at[kind, n],
            recv_sem=kr_sem.at[kind, n],
            device_id={"blk": to},
            device_id_type=MESH,
        )

    def kv_wait(f, n, core, kind):
        ref = kv.at[f, key_rows(n, core)]
        pltpu.make_async_copy(ref, ref, kr_sem.at[kind, n]).wait()

    def project(n):
        _, _, pieces = batches[n]
        parts = [hid[slot, start : start + rows] for slot, start, rows, _, _ in pieces]
        x = parts[0] if len(parts) == 1 else jnp.concatenate(parts, axis=0)
        def normed(piece, j):
            mean_sq = jnp.mean(piece * piece, axis=-1, keepdims=True)
            return piece * lax.rsqrt(mean_sq + 1e-06) * gains[j : j + 1, :]

        def bias_of(j):
            return bias[j : j + 1, :].astype(jnp.float32)

        if n == 0:
            w_in[0].wait()
            w_in[1].wait()
        both = jnp.concatenate([wv[1], wv[2]], axis=1)
        made = jnp.dot(x, both, preferred_element_type=jnp.float32)
        made = made + jnp.concatenate([bias_of(1), bias_of(2)], axis=1)
        for g in range(2 * heads):
            piece = made[:, g * HD : (g + 1) * HD]
            if g < heads:
                piece = normed(piece, 1)
            kv[1, key_rows(n, c), g * HD : (g + 1) * HD] = piece.astype(jnp.bfloat16)
        kv_copy(1, 2, n, down, 2).start()
        kv_copy(1, 0, n, up, 1).start()
        kv_copy(1, 1, n, partner, 0).start()
        if n == 0:
            w_in[2].wait()
        made = jnp.dot(x, wv[0], preferred_element_type=jnp.float32) + bias_of(0)
        for g in range(heads):
            cols = slice(g * HD, (g + 1) * HD)
            piece = normed(made[:, cols], 0).astype(jnp.bfloat16)
            at = 0
            for _, _, rows, block, start in pieces:
                qb[block, start : start + rows, cols] = piece[at : at + rows]
                at += rows

    def relay(n):
        kv_wait(0, n, c, 1)
        kv_copy(0, 0, n, partner, 3).start()
        kv_wait(2, n, c, 2)
        kv_copy(2, 2, n, partner, 4).start()

    def near(n):
        kv_wait(1, n, 1 - c, 0)

    def far(n):
        kv_wait(0, n, 1 - c, 3)
        kv_wait(2, n, 1 - c, 4)

    own_in.wait()
    small[0].wait()
    small[1].wait()
    project(0)
    small[2].wait()
    small[3].wait()

    def check_row(t, bad):
        n = counts[t]
        for s in range(slots):
            gap = lax.rem(lists[s, t] // 4 - t // 4 + n_z, n_z)
            far_one = jnp.where((gap > 1) & (gap < n_z - 1) & (s < n), 1, 0)
            bad = jnp.maximum(bad, far_one)
        return bad

    bad = lax.fori_loop(0, n_tiles, check_row, jnp.int32(0))
    flags[0] = jnp.full(flags.shape[1:], bad, jnp.int32)

    def mask_entry(i, carry):
        q = i // 12
        f = lax.rem(i // 4, 3)
        kt = lax.rem(i // 2, 2)
        core = lax.rem(i, 2)
        row = 2 * b + lax.rem(t0 + q, 2)
        tile = 4 * lax.rem(z + f + n_z - 1, n_z) + 2 * core + lax.rem(t0 + kt, 2)
        n = counts[row]
        hit = jnp.int32(0)
        for s in range(slots):
            hit = jnp.maximum(hit, jnp.where((lists[s, row] == tile) & (s < n), 1, 0))
        mask[i] = hit.astype(jnp.float32)
        return carry

    lax.fori_loop(0, 24, mask_entry, 0)

    def flag_send(src, dst, to, k):
        return pltpu.make_async_remote_copy(
            src_ref=flags.at[src],
            dst_ref=flags.at[dst],
            send_sem=fs_sem.at[k],
            recv_sem=fr_sem.at[k],
            device_id={"dp": to},
            device_id_type=MESH,
        )

    flag_sends = [flag_send(0, 1, d_up, 0), flag_send(0, 2, d_down, 1), flag_send(3, 4, d_up, 2)]
    flag_sends[0].start()
    flag_sends[1].start()

    def flag_wait(dst, k):
        ref = flags.at[dst]
        pltpu.make_async_copy(ref, ref, fr_sem.at[k]).wait()

    acc[...] = jnp.zeros_like(acc)

    mixed = [(half, 1 - mate_left), (half, mate_left)]
    segments = [[(chunk, 0)], mixed, mixed, [(2 * part, 1)], [(2 * rest, 1)]]

    def attend(block, count, tile, groups, joined=False):
        spans = []
        for f, group in groups:
            base = tile * 12 + f * 4
            live = jnp.concatenate(
                [
                    jnp.full((rows, HD), mask[base + kt * 2 + core], jnp.float32)
                    for n in group
                    for core in range(2)
                    for rows, kt in segments[n]
                ],
                axis=0,
            ).astype(jnp.bfloat16)
            first = batches[group[0]][0]
            spans.append((f, slice(first, first + live.shape[0]), live))
        rows = pl.ds(block, count)
        for g in range(heads):
            qh = qb[rows, :, g * HD : (g + 1) * HD].reshape(count * chunk, HD)
            pieces = [
                (
                    kv[f, keys, g * HD : (g + 1) * HD],
                    jnp.concatenate(
                        [kv[f, keys, width + g * HD : width + (g + 1) * HD] * live, live], axis=1
                    ),
                )
                for f, keys, live in spans
            ]
            if joined:
                pieces = [tuple(jnp.concatenate(part, axis=0) for part in zip(*pieces))]
            added = None
            for kh, ext in pieces:
                score = lax.dot_general(
                    qh, kh, (((1,), (1,)), ((), ())), preferred_element_type=jnp.float32
                )
                w = jnp.exp(score * HD ** (-0.5)).astype(jnp.bfloat16)
                term = jnp.dot(w, ext, preferred_element_type=jnp.float32)
                added = term if added is None else added + term
            acc[rows, g] += added.reshape(count, chunk, 2 * HD)

    def finish(block):
        for g in range(heads):
            full = acc[block, g]
            ob[block, :, g * HD : (g + 1) * HD] = (full[:, :HD] / full[:, HD:]).astype(jnp.bfloat16)

    def columns(p):
        return pl.ds(pl.multiple_of(p * width, width), width)

    def out_send(src, dst, to, k):
        return pltpu.make_async_remote_copy(
            src_ref=src,
            dst_ref=dst,
            send_sem=os_sem.at[k],
            recv_sem=or_sem.at[k],
            device_id={"head": to},
            device_id_type=MESH,
        )

    upper, lower = pl.ds(0, half), pl.ds(half, half)
    out_sends = [
        out_send(ob.at[3, upper], passing.at[0], right, 0),
        out_send(ob.at[3, lower], passing.at[1], left, 1),
        out_send(ob.at[2], out.at[:, columns(h)], other, 2),
        out_send(ob.at[1], out.at[:, columns(h)], mate, 3),
        out_send(passing.at[0], out.at[upper, columns(left)], right, 4),
        out_send(passing.at[1], out.at[lower, columns(right)], left, 5),
    ]
    own_out = pltpu.make_async_copy(ob.at[0], out.at[:, columns(h)], own_sem)

    hid_wait(1, 0, half, 0)
    hops[4].start()
    hops[6].start()
    hid_wait(2, half, half, 4)
    hops[5].start()
    hops[7].start()
    relay(0)
    project(1)
    flag_wait(1, 0)
    flags[3] = jnp.maximum(flags[0], flags[1])
    flag_sends[2].start()
    near(0)
    near(1)

    def own_first(i, carry):
        @pl.when(i == 1)
        def _():
            relay(1)
            far(0)
            far(1)

        attend(0, 1, 0, [(lax.rem(2 * i + 1, 3), (0, 1))])
        return carry

    lax.fori_loop(0, 3, own_first, 0)
    flag_wait(2, 1)
    flag_wait(4, 2)
    seen = jnp.maximum(jnp.maximum(flags[2], flags[3]), flags[4])
    flag_out[...] = seen[0:1, 0:1]
    hid_wait(1, half, half, 1)
    hid_wait(2, 0, half, 5)
    project(2)

    def neighbours_first(i, carry):
        attend(1 + i, 1, i, [(f, (0, 1)) for f in range(3)])
        return carry

    lax.fori_loop(0, 2, neighbours_first, 0)
    hid_wait(3, 0, part, 2)
    hid_wait(3, chunk - part, part, 6)
    project(3)
    relay(2)
    near(2)
    far(2)
    attend(0, 2, 0, [(f, (2,)) for f in range(3)], True)
    hid_wait(3, part, rest, 3)
    hid_wait(3, half, rest, 7)
    project(4)
    attend(3, 1, 1, [(f, (0, 1)) for f in range(3)])
    keep = [pltpu.make_async_copy(qb, q_out, x_sem.at[5])]
    at = 0
    for n, (_, rows, _) in enumerate(batches):
        keep.append(pltpu.make_async_copy(kv.at[1, key_rows(n, c)], kv_out.at[pl.ds(at, rows)], x_sem.at[n]))
        at += rows
    for copy in keep:
        copy.start()
    relay(3)
    attend(2, 2, 1, [(f, (2,)) for f in range(3)], True)
    near(3)
    far(3)
    relay(4)
    attend(2, 2, 1, [(f, (3,)) for f in range(3)], True)
    near(4)
    far(4)
    attend(2, 2, 1, [(f, (4,)) for f in range(3)], True)
    finish(3)
    out_sends[0].start()
    out_sends[1].start()
    finish(2)
    out_sends[2].start()
    attend(0, 2, 0, [(f, (3, 4)) for f in range(3)], True)
    finish(1)
    out_sends[3].start()
    finish(0)
    own_out.start()
    for k in range(2):
        ref = passing.at[k]
        pltpu.make_async_copy(ref, ref, or_sem.at[k]).wait()
        out_sends[4 + k].start()

    for copy in hops:
        copy.wait_send()
    for n in range(5):
        kv_copy(1, 1, n, partner, 0).wait_send()
        kv_copy(1, 0, n, up, 1).wait_send()
        kv_copy(1, 2, n, down, 2).wait_send()
        kv_copy(0, 0, n, partner, 3).wait_send()
        kv_copy(2, 2, n, partner, 4).wait_send()
    for copy in flag_sends:
        copy.wait_send()
    for copy in keep:
        copy.wait()
    own_out.wait()
    for copy in out_sends:
        copy.wait_send()
    for k, ref in (
        (2, out.at[:, columns(other)]),
        (3, out.at[:, columns(mate)]),
        (4, out.at[upper, columns(opp)]),
        (5, out.at[lower, columns(opp)]),
    ):
        pltpu.make_async_copy(ref, ref, or_sem.at[k]).wait()


def window_attention(hidden, weight, bias, gains, lists, counts):
    n_blk = lax.axis_size("blk")
    n_dp = lax.axis_size("dp")
    chunk, depth = hidden.shape
    width = weight.shape[2]
    heads = width // HD
    slots, n_tiles = lists.shape
    sizes = (n_blk, n_dp, heads, slots, n_tiles)
    hbm = pl.BlockSpec(memory_space=pl.ANY)
    vmem = pl.BlockSpec(memory_space=pltpu.VMEM)
    dma = pltpu.SemaphoreType.DMA
    return pl.pallas_call(
        functools.partial(kernel, sizes),
        out_shape=(
            jax.ShapeDtypeStruct((chunk, 4 * width), jnp.bfloat16),
            jax.ShapeDtypeStruct((4, chunk, width), jnp.bfloat16),
            jax.ShapeDtypeStruct((4 * chunk, 2 * width), jnp.bfloat16),
            jax.ShapeDtypeStruct((1, 1), jnp.int32),
        ),
        in_specs=[hbm] * 6,
        out_specs=(hbm, hbm, hbm, vmem),
        scratch_shapes=[
            pltpu.VMEM((4, chunk, depth), jnp.bfloat16),
            pltpu.VMEM((3, depth, width), jnp.bfloat16),
            pltpu.VMEM((4, chunk, width), jnp.bfloat16),
            pltpu.VMEM((3, 8 * chunk, 2 * width), jnp.bfloat16),
            pltpu.VMEM((4, heads, chunk, 2 * HD), jnp.float32),
            pltpu.VMEM((4, chunk, width), jnp.bfloat16),
            pltpu.VMEM((2, chunk // 2, width), jnp.bfloat16),
            pltpu.VMEM((5, 8, 128), jnp.int32),
            pltpu.SMEM((24,), jnp.float32),
            pltpu.VMEM(bias.shape, bias.dtype),
            pltpu.VMEM(gains.shape, gains.dtype),
            pltpu.SMEM(lists.shape, lists.dtype),
            pltpu.SMEM(counts.shape, counts.dtype),
            dma,
            dma((3,)),
            dma((8,)),
            dma((8,)),
            dma((5, 5)),
            dma((5, 5)),
            dma((6,)),
            dma((6,)),
            dma((3,)),
            dma((3,)),
            dma((6,)),
            dma((4,)),
        ],
        compiler_params=pltpu.CompilerParams(
            collective_id=0, has_side_effects=True, vmem_limit_bytes=60 * 1024 * 1024
        ),
    )(hidden, weight, bias, gains, lists, counts)


def any_lists(query, key_value, tile_lists, tile_counts):
    n_blk = lax.axis_size("blk")
    place = lax.axis_index("blk")
    h = lax.axis_index("head")
    chunk, width = query.shape[1:]
    heads = width // HD
    rows = 2 * TILE
    half, part = chunk // 2, chunk // 3

    def in_order(own, right, opposite, left):
        around = jnp.concatenate([own, right, opposite, left] * 2, axis=0)
        return lax.dynamic_slice_in_dim(around, lax.rem(4 - h, 4) * chunk, rows, 0)

    odd = lax.rem(h, 2) == 1
    right_q = jnp.where(odd, query[2], query[1])
    left_q = jnp.where(odd, query[1], query[2])
    query = in_order(query[0], right_q, query[3], left_q).reshape(rows, heads, HD)
    one, two, opp = (key_value[i * chunk : (i + 1) * chunk] for i in (1, 2, 3))
    current = in_order(
        key_value[:chunk],
        jnp.concatenate([two[half:], one[half:]], axis=0),
        jnp.concatenate([opp[:part], opp[2 * part :], opp[part : 2 * part]], axis=0),
        jnp.concatenate([one[:half], two[:half]], axis=0),
    )
    lists = lax.dynamic_slice_in_dim(tile_lists, place * 2, 2, 0)
    counts = lax.dynamic_slice_in_dim(tile_counts, place * 2, 2, 0)
    live = jnp.arange(lists.shape[1], dtype=jnp.int32)[None, :] < counts[:, None]
    route = [(i, (i - 1) % n_blk) for i in range(n_blk)]

    def turn(step, carry):
        total, numer, block = carry
        key_tile = 2 * ((place + step) % n_blk) + jnp.arange(rows, dtype=jnp.int32) // TILE
        hits = (lists[:, :, None] == key_tile[None, None, :]) & live[:, :, None]
        mask = jnp.repeat(jnp.any(hits, axis=1), TILE, axis=0)
        keys = block[:, :width].reshape(rows, heads, HD)
        values = block[:, width:].reshape(rows, heads, HD)
        score = jnp.einsum("qhd,khd->hqk", query, keys, preferred_element_type=jnp.float32)
        w = jnp.where(mask[None], jnp.exp(score * HD ** (-0.5)), jnp.float32(0.0))
        total = total + jnp.sum(w, axis=-1)
        numer = numer + jnp.einsum(
            "hqk,khd->hqd", w.astype(jnp.bfloat16), values, preferred_element_type=jnp.float32
        )
        return (total, numer, lax.ppermute(block, "blk", route))

    total, numer, current = lax.fori_loop(
        0,
        n_blk,
        turn,
        (
            jnp.zeros((heads, rows), jnp.float32),
            jnp.zeros((heads, rows, HD), jnp.float32),
            current,
        ),
    )
    attended = (numer / total[:, :, None]).transpose(1, 0, 2).reshape(rows, width)
    return lax.all_to_all(
        attended.astype(jnp.bfloat16), "head", split_axis=0, concat_axis=1, tiled=True
    )


def shards(hidden, qkv_weight, qkv_bias, norm_gains, tile_lists, tile_counts):
    out, query, key_value, flag = window_attention(
        hidden, qkv_weight, qkv_bias, norm_gains, tile_lists.T, tile_counts
    )
    return lax.cond(
        flag[0, 0] > 0,
        lambda: any_lists(query, key_value, tile_lists, tile_counts),
        lambda: out,
    )


def solution(mesh):
    return jax.shard_map(
        shards,
        mesh=mesh,
        in_specs=(
            P(("dp", "blk", "head"), None),
            P(None, None, "head"),
            P(None, "head"),
            P(),
            P("dp", None),
            P("dp"),
        ),
        out_specs=P(("dp", "blk", "head"), None),
        check_vma=False,
    )
```

```python
import functools

import jax
import jax.numpy as jnp
from jax import lax
from jax.experimental import pallas as pl
from jax.experimental.pallas import tpu as pltpu
from jax.sharding import PartitionSpec as P

HD = 128
TILE = 384
MESH = pl.DeviceIdType.MESH


def kernel(
    sizes,
    hidden, weight, bias_in, gains_in, lists_in, counts_in,
    out, q_out, kv_out, flag_out,
    hid, wv, qb, kv, acc, ob, passing, flags, mask,
    bias, gains, lists, counts,
    own_sem, w_sem, hs_sem, hr_sem, ks_sem, kr_sem, os_sem, or_sem, fs_sem, fr_sem, x_sem, s_sem,
):
    n_blk, n_dp, heads, slots, n_tiles = sizes
    chunk = hid.shape[1]
    half = chunk // 2
    part = chunk // 3
    rest = half - part
    width = heads * HD
    b = lax.axis_index("blk")
    h = lax.axis_index("head")
    d = lax.axis_index("dp")
    c = lax.rem(b, 2)
    z = lax.div(b, 2)
    n_z = n_blk // 2
    right = lax.rem(h + 1, 4)
    opp = lax.rem(h + 2, 4)
    left = lax.rem(h + 3, 4)
    hb = lax.rem(h, 2)
    t0 = lax.div(h, 2)
    mate = h + 1 - 2 * hb
    other = lax.rem(h + 3 + 2 * hb, 4)
    partner = b + 1 - 2 * c
    up = lax.rem(b + 2, n_blk)
    down = lax.rem(b + n_blk - 2, n_blk)
    d_up = lax.rem(d + 1, n_dp)
    d_down = lax.rem(d + n_dp - 1, n_dp)

    barrier = pltpu.get_barrier_semaphore()
    for p in (right, left):
        pl.semaphore_signal(barrier, inc=1, device_id={"head": p}, device_id_type=MESH)
    for p in (up, down, partner):
        pl.semaphore_signal(barrier, inc=1, device_id={"blk": p}, device_id_type=MESH)
    for p in (d_up, d_down):
        pl.semaphore_signal(barrier, inc=1, device_id={"dp": p}, device_id_type=MESH)
    own_in = pltpu.make_async_copy(hidden, hid.at[0], own_sem)
    own_in.start()
    w_in = [pltpu.make_async_copy(weight.at[j], wv.at[j], w_sem.at[j]) for j in (1, 2, 0)]
    for copy in w_in:
        copy.start()
    small = [
        pltpu.make_async_copy(src, dst, s_sem.at[k])
        for k, (src, dst) in enumerate(
            ((bias_in, bias), (gains_in, gains), (lists_in, lists), (counts_in, counts))
        )
    ]
    for copy in small:
        copy.start()
    pl.semaphore_wait(barrier, 7)

    def hid_send(src, slot, start, rows, to, k):
        return pltpu.make_async_remote_copy(
            src_ref=src.at[pl.ds(start, rows)],
            dst_ref=hid.at[slot, pl.ds(start, rows)],
            send_sem=hs_sem.at[k],
            recv_sem=hr_sem.at[k],
            device_id={"head": to},
            device_id_type=MESH,
        )

    hops = [
        hid_send(hidden, 1, 0, half, right, 0),
        hid_send(hidden, 2, half, half, left, 4),
        hid_send(hidden, 1, half, half, right, 1),
        hid_send(hidden, 2, 0, half, left, 5),
        hid_send(hid.at[1], 3, 0, part, right, 2),
        hid_send(hid.at[2], 3, chunk - part, part, left, 6),
        hid_send(hid.at[1], 3, part, rest, right, 3),
        hid_send(hid.at[2], 3, half, rest, left, 7),
    ]
    for copy in hops[:4]:
        copy.start()

    def hid_wait(slot, start, rows, k):
        ref = hid.at[slot, pl.ds(start, rows)]
        pltpu.make_async_copy(ref, ref, hr_sem.at[k]).wait()

    mate_left = hb
    left_block = 2 - mate_left
    right_block = 1 + mate_left
    batches = [
        (0, chunk, [(0, 0, chunk, 0, 0)]),
        (2 * chunk, chunk, [(1, 0, half, left_block, 0), (2, half, half, right_block, half)]),
        (4 * chunk, chunk, [(1, half, half, left_block, half), (2, 0, half, right_block, 0)]),
        (6 * chunk, 2 * part, [(3, 0, part, 3, 0), (3, chunk - part, part, 3, chunk - part)]),
        (6 * chunk + 4 * part, 2 * rest, [(3, part, 2 * rest, 3, part)]),
    ]

    def key_rows(n, core):
        first, rows, _ = batches[n]
        return pl.ds(pl.multiple_of(first + core * rows, rows), rows)

    def kv_copy(src_f, dst_f, n, to, kind):
        rows = key_rows(n, c)
        return pltpu.make_async_remote_copy(
            src_ref=kv.at[src_f, rows],
            dst_ref=kv.at[dst_f, rows],
            send_sem=ks_sem.at[kind, n],
            recv_sem=kr_sem.at[kind, n],
            device_id={"blk": to},
            device_id_type=MESH,
        )

    def kv_wait(f, n, core, kind):
        ref = kv.at[f, key_rows(n, core)]
        pltpu.make_async_copy(ref, ref, kr_sem.at[kind, n]).wait()

    def project(n):
        _, _, pieces = batches[n]
        parts = [hid[slot, start : start + rows] for slot, start, rows, _, _ in pieces]
        x = parts[0] if len(parts) == 1 else jnp.concatenate(parts, axis=0)
        def normed(piece, j):
            mean_sq = jnp.mean(piece * piece, axis=-1, keepdims=True)
            return piece * lax.rsqrt(mean_sq + 1e-06) * gains[j : j + 1, :]

        def bias_of(j):
            return bias[j : j + 1, :].astype(jnp.float32)

        if n == 0:
            w_in[0].wait()
            w_in[1].wait()
        both = jnp.concatenate([wv[1], wv[2]], axis=1)
        made = jnp.dot(x, both, preferred_element_type=jnp.float32)
        made = made + jnp.concatenate([bias_of(1), bias_of(2)], axis=1)
        for g in range(2 * heads):
            piece = made[:, g * HD : (g + 1) * HD]
            if g < heads:
                piece = normed(piece, 1)
            kv[1, key_rows(n, c), g * HD : (g + 1) * HD] = piece.astype(jnp.bfloat16)
        kv_copy(1, 2, n, down, 2).start()
        kv_copy(1, 0, n, up, 1).start()
        kv_copy(1, 1, n, partner, 0).start()
        if n == 0:
            w_in[2].wait()
        made = jnp.dot(x, wv[0], preferred_element_type=jnp.float32) + bias_of(0)
        for g in range(heads):
            cols = slice(g * HD, (g + 1) * HD)
            piece = normed(made[:, cols], 0).astype(jnp.bfloat16)
            at = 0
            for _, _, rows, block, start in pieces:
                qb[block, start : start + rows, cols] = piece[at : at + rows]
                at += rows

    def relay(n):
        kv_wait(0, n, c, 1)
        kv_copy(0, 0, n, partner, 3).start()
        kv_wait(2, n, c, 2)
        kv_copy(2, 2, n, partner, 4).start()

    def near(n):
        kv_wait(1, n, 1 - c, 0)

    def far(n):
        kv_wait(0, n, 1 - c, 3)
        kv_wait(2, n, 1 - c, 4)

    own_in.wait()
    small[0].wait()
    small[1].wait()
    project(0)
    small[2].wait()
    small[3].wait()

    def check_row(t, bad):
        n = counts[t]
        for s in range(slots):
            gap = lax.rem(lists[s, t] // 4 - t // 4 + n_z, n_z)
            far_one = jnp.where((gap > 1) & (gap < n_z - 1) & (s < n), 1, 0)
            bad = jnp.maximum(bad, far_one)
        return bad

    bad = lax.fori_loop(0, n_tiles, check_row, jnp.int32(0))
    flags[0] = jnp.full(flags.shape[1:], bad, jnp.int32)

    def mask_entry(i, carry):
        q = i // 12
        f = lax.rem(i // 4, 3)
        kt = lax.rem(i // 2, 2)
        core = lax.rem(i, 2)
        row = 2 * b + lax.rem(t0 + q, 2)
        tile = 4 * lax.rem(z + f + n_z - 1, n_z) + 2 * core + lax.rem(t0 + kt, 2)
        n = counts[row]
        hit = jnp.int32(0)
        for s in range(slots):
            hit = jnp.maximum(hit, jnp.where((lists[s, row] == tile) & (s < n), 1, 0))
        mask[i] = hit.astype(jnp.float32)
        return carry

    lax.fori_loop(0, 24, mask_entry, 0)

    def flag_send(src, dst, to, k):
        return pltpu.make_async_remote_copy(
            src_ref=flags.at[src],
            dst_ref=flags.at[dst],
            send_sem=fs_sem.at[k],
            recv_sem=fr_sem.at[k],
            device_id={"dp": to},
            device_id_type=MESH,
        )

    flag_sends = [flag_send(0, 1, d_up, 0), flag_send(0, 2, d_down, 1), flag_send(3, 4, d_up, 2)]
    flag_sends[0].start()
    flag_sends[1].start()

    def flag_wait(dst, k):
        ref = flags.at[dst]
        pltpu.make_async_copy(ref, ref, fr_sem.at[k]).wait()

    acc[...] = jnp.zeros_like(acc)

    mixed = [(half, 1 - mate_left), (half, mate_left)]
    segments = [[(chunk, 0)], mixed, mixed, [(2 * part, 1)], [(2 * rest, 1)]]

    def attend(block, count, tile, groups, joined=False):
        spans = []
        for f, group in groups:
            base = tile * 12 + f * 4
            live = jnp.concatenate(
                [
                    jnp.full((rows, HD), mask[base + kt * 2 + core], jnp.float32)
                    for n in group
                    for core in range(2)
                    for rows, kt in segments[n]
                ],
                axis=0,
            ).astype(jnp.bfloat16)
            first = batches[group[0]][0]
            spans.append((f, slice(first, first + live.shape[0]), live))
        rows = pl.ds(block, count)
        for g in range(heads):
            qh = qb[rows, :, g * HD : (g + 1) * HD].reshape(count * chunk, HD)
            pieces = [
                (
                    kv[f, keys, g * HD : (g + 1) * HD],
                    jnp.concatenate(
                        [kv[f, keys, width + g * HD : width + (g + 1) * HD] * live, live], axis=1
                    ),
                )
                for f, keys, live in spans
            ]
            if joined:
                pieces = [tuple(jnp.concatenate(part, axis=0) for part in zip(*pieces))]
            added = None
            for kh, ext in pieces:
                score = lax.dot_general(
                    qh, kh, (((1,), (1,)), ((), ())), preferred_element_type=jnp.float32
                )
                w = jnp.exp(score * HD ** (-0.5)).astype(jnp.bfloat16)
                term = jnp.dot(w, ext, preferred_element_type=jnp.float32)
                added = term if added is None else added + term
            acc[rows, g] += added.reshape(count, chunk, 2 * HD)

    def finish(block):
        for g in range(heads):
            full = acc[block, g]
            ob[block, :, g * HD : (g + 1) * HD] = (full[:, :HD] / full[:, HD:]).astype(jnp.bfloat16)

    def columns(p):
        return pl.ds(pl.multiple_of(p * width, width), width)

    def out_send(src, dst, to, k):
        return pltpu.make_async_remote_copy(
            src_ref=src,
            dst_ref=dst,
            send_sem=os_sem.at[k],
            recv_sem=or_sem.at[k],
            device_id={"head": to},
            device_id_type=MESH,
        )

    upper, lower = pl.ds(0, half), pl.ds(half, half)
    out_sends = [
        out_send(ob.at[3, upper], passing.at[0], right, 0),
        out_send(ob.at[3, lower], passing.at[1], left, 1),
        out_send(ob.at[2], out.at[:, columns(h)], other, 2),
        out_send(ob.at[1], out.at[:, columns(h)], mate, 3),
        out_send(passing.at[0], out.at[upper, columns(left)], right, 4),
        out_send(passing.at[1], out.at[lower, columns(right)], left, 5),
    ]
    own_out = pltpu.make_async_copy(ob.at[0], out.at[:, columns(h)], own_sem)

    hid_wait(1, 0, half, 0)
    hops[4].start()
    hops[6].start()
    hid_wait(2, half, half, 4)
    hops[5].start()
    hops[7].start()
    relay(0)
    project(1)
    flag_wait(1, 0)
    flags[3] = jnp.maximum(flags[0], flags[1])
    flag_sends[2].start()
    near(0)
    near(1)

    def own_first(i, carry):
        @pl.when(i == 1)
        def _():
            relay(1)
            far(0)
            far(1)

        attend(0, 1, 0, [(lax.rem(2 * i + 1, 3), (0, 1))])
        return carry

    lax.fori_loop(0, 3, own_first, 0)
    flag_wait(2, 1)
    flag_wait(4, 2)
    seen = jnp.maximum(jnp.maximum(flags[2], flags[3]), flags[4])
    flag_out[...] = seen[0:1, 0:1]
    hid_wait(1, half, half, 1)
    hid_wait(2, 0, half, 5)
    project(2)

    def neighbours_first(i, carry):
        attend(1 + i, 1, i, [(f, (0, 1)) for f in range(3)])
        return carry

    lax.fori_loop(0, 2, neighbours_first, 0)
    near(2)
    attend(0, 2, 0, [(1, (2,))])
    attend(2, 1, 1, [(1, (2,))])
    hid_wait(3, 0, part, 2)
    hid_wait(3, chunk - part, part, 6)
    project(3)
    relay(2)
    far(2)
    attend(0, 2, 0, [(0, (2,)), (2, (2,))], True)
    attend(2, 1, 1, [(0, (2,)), (2, (2,))], True)
    hid_wait(3, part, rest, 3)
    hid_wait(3, half, rest, 7)
    project(4)
    attend(3, 1, 1, [(f, (0, 1)) for f in range(3)])
    keep = [pltpu.make_async_copy(qb, q_out, x_sem.at[5])]
    at = 0
    for n, (_, rows, _) in enumerate(batches):
        keep.append(pltpu.make_async_copy(kv.at[1, key_rows(n, c)], kv_out.at[pl.ds(at, rows)], x_sem.at[n]))
        at += rows
    for copy in keep:
        copy.start()
    relay(3)
    attend(3, 1, 1, [(f, (2,)) for f in range(3)], True)
    near(3)
    far(3)
    relay(4)
    attend(2, 2, 1, [(f, (3,)) for f in range(3)], True)
    near(4)
    far(4)
    attend(2, 2, 1, [(f, (4,)) for f in range(3)], True)
    finish(3)
    out_sends[0].start()
    out_sends[1].start()
    finish(2)
    out_sends[2].start()
    attend(0, 2, 0, [(f, (3, 4)) for f in range(3)], True)
    finish(1)
    out_sends[3].start()
    finish(0)
    own_out.start()
    for k in range(2):
        ref = passing.at[k]
        pltpu.make_async_copy(ref, ref, or_sem.at[k]).wait()
        out_sends[4 + k].start()

    for copy in hops:
        copy.wait_send()
    for n in range(5):
        kv_copy(1, 1, n, partner, 0).wait_send()
        kv_copy(1, 0, n, up, 1).wait_send()
        kv_copy(1, 2, n, down, 2).wait_send()
        kv_copy(0, 0, n, partner, 3).wait_send()
        kv_copy(2, 2, n, partner, 4).wait_send()
    for copy in flag_sends:
        copy.wait_send()
    for copy in keep:
        copy.wait()
    own_out.wait()
    for copy in out_sends:
        copy.wait_send()
    for k, ref in (
        (2, out.at[:, columns(other)]),
        (3, out.at[:, columns(mate)]),
        (4, out.at[upper, columns(opp)]),
        (5, out.at[lower, columns(opp)]),
    ):
        pltpu.make_async_copy(ref, ref, or_sem.at[k]).wait()


def window_attention(hidden, weight, bias, gains, lists, counts):
    n_blk = lax.axis_size("blk")
    n_dp = lax.axis_size("dp")
    chunk, depth = hidden.shape
    width = weight.shape[2]
    heads = width // HD
    slots, n_tiles = lists.shape
    sizes = (n_blk, n_dp, heads, slots, n_tiles)
    hbm = pl.BlockSpec(memory_space=pl.ANY)
    vmem = pl.BlockSpec(memory_space=pltpu.VMEM)
    dma = pltpu.SemaphoreType.DMA
    return pl.pallas_call(
        functools.partial(kernel, sizes),
        out_shape=(
            jax.ShapeDtypeStruct((chunk, 4 * width), jnp.bfloat16),
            jax.ShapeDtypeStruct((4, chunk, width), jnp.bfloat16),
            jax.ShapeDtypeStruct((4 * chunk, 2 * width), jnp.bfloat16),
            jax.ShapeDtypeStruct((1, 1), jnp.int32),
        ),
        in_specs=[hbm] * 6,
        out_specs=(hbm, hbm, hbm, vmem),
        scratch_shapes=[
            pltpu.VMEM((4, chunk, depth), jnp.bfloat16),
            pltpu.VMEM((3, depth, width), jnp.bfloat16),
            pltpu.VMEM((4, chunk, width), jnp.bfloat16),
            pltpu.VMEM((3, 8 * chunk, 2 * width), jnp.bfloat16),
            pltpu.VMEM((4, heads, chunk, 2 * HD), jnp.float32),
            pltpu.VMEM((4, chunk, width), jnp.bfloat16),
            pltpu.VMEM((2, chunk // 2, width), jnp.bfloat16),
            pltpu.VMEM((5, 8, 128), jnp.int32),
            pltpu.SMEM((24,), jnp.float32),
            pltpu.VMEM(bias.shape, bias.dtype),
            pltpu.VMEM(gains.shape, gains.dtype),
            pltpu.SMEM(lists.shape, lists.dtype),
            pltpu.SMEM(counts.shape, counts.dtype),
            dma,
            dma((3,)),
            dma((8,)),
            dma((8,)),
            dma((5, 5)),
            dma((5, 5)),
            dma((6,)),
            dma((6,)),
            dma((3,)),
            dma((3,)),
            dma((6,)),
            dma((4,)),
        ],
        compiler_params=pltpu.CompilerParams(
            collective_id=0, has_side_effects=True, vmem_limit_bytes=60 * 1024 * 1024
        ),
    )(hidden, weight, bias, gains, lists, counts)


def any_lists(query, key_value, tile_lists, tile_counts):
    n_blk = lax.axis_size("blk")
    place = lax.axis_index("blk")
    h = lax.axis_index("head")
    chunk, width = query.shape[1:]
    heads = width // HD
    rows = 2 * TILE
    half, part = chunk // 2, chunk // 3

    def in_order(own, right, opposite, left):
        around = jnp.concatenate([own, right, opposite, left] * 2, axis=0)
        return lax.dynamic_slice_in_dim(around, lax.rem(4 - h, 4) * chunk, rows, 0)

    odd = lax.rem(h, 2) == 1
    right_q = jnp.where(odd, query[2], query[1])
    left_q = jnp.where(odd, query[1], query[2])
    query = in_order(query[0], right_q, query[3], left_q).reshape(rows, heads, HD)
    one, two, opp = (key_value[i * chunk : (i + 1) * chunk] for i in (1, 2, 3))
    current = in_order(
        key_value[:chunk],
        jnp.concatenate([two[half:], one[half:]], axis=0),
        jnp.concatenate([opp[:part], opp[2 * part :], opp[part : 2 * part]], axis=0),
        jnp.concatenate([one[:half], two[:half]], axis=0),
    )
    lists = lax.dynamic_slice_in_dim(tile_lists, place * 2, 2, 0)
    counts = lax.dynamic_slice_in_dim(tile_counts, place * 2, 2, 0)
    live = jnp.arange(lists.shape[1], dtype=jnp.int32)[None, :] < counts[:, None]
    route = [(i, (i - 1) % n_blk) for i in range(n_blk)]

    def turn(step, carry):
        total, numer, block = carry
        key_tile = 2 * ((place + step) % n_blk) + jnp.arange(rows, dtype=jnp.int32) // TILE
        hits = (lists[:, :, None] == key_tile[None, None, :]) & live[:, :, None]
        mask = jnp.repeat(jnp.any(hits, axis=1), TILE, axis=0)
        keys = block[:, :width].reshape(rows, heads, HD)
        values = block[:, width:].reshape(rows, heads, HD)
        score = jnp.einsum("qhd,khd->hqk", query, keys, preferred_element_type=jnp.float32)
        w = jnp.where(mask[None], jnp.exp(score * HD ** (-0.5)), jnp.float32(0.0))
        total = total + jnp.sum(w, axis=-1)
        numer = numer + jnp.einsum(
            "hqk,khd->hqd", w.astype(jnp.bfloat16), values, preferred_element_type=jnp.float32
        )
        return (total, numer, lax.ppermute(block, "blk", route))

    total, numer, current = lax.fori_loop(
        0,
        n_blk,
        turn,
        (
            jnp.zeros((heads, rows), jnp.float32),
            jnp.zeros((heads, rows, HD), jnp.float32),
            current,
        ),
    )
    attended = (numer / total[:, :, None]).transpose(1, 0, 2).reshape(rows, width)
    return lax.all_to_all(
        attended.astype(jnp.bfloat16), "head", split_axis=0, concat_axis=1, tiled=True
    )


def shards(hidden, qkv_weight, qkv_bias, norm_gains, tile_lists, tile_counts):
    out, query, key_value, flag = window_attention(
        hidden, qkv_weight, qkv_bias, norm_gains, tile_lists.T, tile_counts
    )
    return lax.cond(
        flag[0, 0] > 0,
        lambda: any_lists(query, key_value, tile_lists, tile_counts),
        lambda: out,
    )


def solution(mesh):
    return jax.shard_map(
        shards,
        mesh=mesh,
        in_specs=(
            P(("dp", "blk", "head"), None),
            P(None, None, "head"),
            P(None, "head"),
            P(),
            P("dp", None),
            P("dp"),
        ),
        out_specs=P(("dp", "blk", "head"), None),
        check_vma=False,
    )
```

```python
import functools

import jax
import jax.numpy as jnp
from jax import lax
from jax.experimental import pallas as pl
from jax.experimental.pallas import tpu as pltpu
from jax.sharding import PartitionSpec as P

HD = 128
TILE = 384
MESH = pl.DeviceIdType.MESH


def kernel(
    sizes,
    hidden, weight, bias_in, gains_in, lists_in, counts_in,
    out, q_out, kv_out, flag_out,
    hid, wv, qb, kv, acc, ob, passing, flags, mask,
    bias, gains, lists, counts,
    own_sem, w_sem, hs_sem, hr_sem, ks_sem, kr_sem, os_sem, or_sem, fs_sem, fr_sem, x_sem, s_sem,
):
    n_blk, n_dp, heads, slots, n_tiles = sizes
    chunk = hid.shape[1]
    half = chunk // 2
    part = chunk // 3
    rest = half - part
    width = heads * HD
    b = lax.axis_index("blk")
    h = lax.axis_index("head")
    d = lax.axis_index("dp")
    c = lax.rem(b, 2)
    z = lax.div(b, 2)
    n_z = n_blk // 2
    right = lax.rem(h + 1, 4)
    opp = lax.rem(h + 2, 4)
    left = lax.rem(h + 3, 4)
    hb = lax.rem(h, 2)
    t0 = lax.div(h, 2)
    mate = h + 1 - 2 * hb
    other = lax.rem(h + 3 + 2 * hb, 4)
    partner = b + 1 - 2 * c
    up = lax.rem(b + 2, n_blk)
    down = lax.rem(b + n_blk - 2, n_blk)
    d_up = lax.rem(d + 1, n_dp)
    d_down = lax.rem(d + n_dp - 1, n_dp)

    barrier = pltpu.get_barrier_semaphore()
    for p in (right, left):
        pl.semaphore_signal(barrier, inc=1, device_id={"head": p}, device_id_type=MESH)
    for p in (up, down, partner):
        pl.semaphore_signal(barrier, inc=1, device_id={"blk": p}, device_id_type=MESH)
    for p in (d_up, d_down):
        pl.semaphore_signal(barrier, inc=1, device_id={"dp": p}, device_id_type=MESH)
    own_in = pltpu.make_async_copy(hidden, hid.at[0], own_sem)
    own_in.start()
    w_in = [pltpu.make_async_copy(weight.at[j], wv.at[j], w_sem.at[j]) for j in (1, 2, 0)]
    for copy in w_in:
        copy.start()
    small = [
        pltpu.make_async_copy(src, dst, s_sem.at[k])
        for k, (src, dst) in enumerate(
            ((bias_in, bias), (gains_in, gains), (lists_in, lists), (counts_in, counts))
        )
    ]
    for copy in small:
        copy.start()
    pl.semaphore_wait(barrier, 7)

    def hid_send(src, slot, start, rows, to, k):
        return pltpu.make_async_remote_copy(
            src_ref=src.at[pl.ds(start, rows)],
            dst_ref=hid.at[slot, pl.ds(start, rows)],
            send_sem=hs_sem.at[k],
            recv_sem=hr_sem.at[k],
            device_id={"head": to},
            device_id_type=MESH,
        )

    hops = [
        hid_send(hidden, 1, 0, half, right, 0),
        hid_send(hidden, 2, half, half, left, 4),
        hid_send(hidden, 1, half, half, right, 1),
        hid_send(hidden, 2, 0, half, left, 5),
        hid_send(hid.at[1], 3, 0, part, right, 2),
        hid_send(hid.at[2], 3, chunk - part, part, left, 6),
        hid_send(hid.at[1], 3, part, rest, right, 3),
        hid_send(hid.at[2], 3, half, rest, left, 7),
    ]
    for copy in hops[:4]:
        copy.start()

    def hid_wait(slot, start, rows, k):
        ref = hid.at[slot, pl.ds(start, rows)]
        pltpu.make_async_copy(ref, ref, hr_sem.at[k]).wait()

    mate_left = hb
    left_block = 2 - mate_left
    right_block = 1 + mate_left
    batches = [
        (0, chunk, [(0, 0, chunk, 0, 0)]),
        (2 * chunk, chunk, [(1, 0, half, left_block, 0), (2, half, half, right_block, half)]),
        (4 * chunk, chunk, [(1, half, half, left_block, half), (2, 0, half, right_block, 0)]),
        (6 * chunk, 2 * part, [(3, 0, part, 3, 0), (3, chunk - part, part, 3, chunk - part)]),
        (6 * chunk + 4 * part, 2 * rest, [(3, part, 2 * rest, 3, part)]),
    ]

    def key_rows(n, core):
        first, rows, _ = batches[n]
        return pl.ds(pl.multiple_of(first + core * rows, rows), rows)

    def kv_copy(src_f, dst_f, n, to, kind):
        rows = key_rows(n, c)
        return pltpu.make_async_remote_copy(
            src_ref=kv.at[src_f, rows],
            dst_ref=kv.at[dst_f, rows],
            send_sem=ks_sem.at[kind, n],
            recv_sem=kr_sem.at[kind, n],
            device_id={"blk": to},
            device_id_type=MESH,
        )

    def kv_wait(f, n, core, kind):
        ref = kv.at[f, key_rows(n, core)]
        pltpu.make_async_copy(ref, ref, kr_sem.at[kind, n]).wait()

    def project(n):
        _, _, pieces = batches[n]
        parts = [hid[slot, start : start + rows] for slot, start, rows, _, _ in pieces]
        x = parts[0] if len(parts) == 1 else jnp.concatenate(parts, axis=0)
        def normed(piece, j):
            mean_sq = jnp.mean(piece * piece, axis=-1, keepdims=True)
            return piece * lax.rsqrt(mean_sq + 1e-06) * gains[j : j + 1, :]

        def bias_of(j):
            return bias[j : j + 1, :].astype(jnp.float32)

        if n == 0:
            w_in[0].wait()
            w_in[1].wait()
        both = jnp.concatenate([wv[1], wv[2]], axis=1)
        made = jnp.dot(x, both, preferred_element_type=jnp.float32)
        made = made + jnp.concatenate([bias_of(1), bias_of(2)], axis=1)
        for g in range(2 * heads):
            piece = made[:, g * HD : (g + 1) * HD]
            if g < heads:
                piece = normed(piece, 1)
            kv[1, key_rows(n, c), g * HD : (g + 1) * HD] = piece.astype(jnp.bfloat16)
        kv_copy(1, 2, n, down, 2).start()
        kv_copy(1, 0, n, up, 1).start()
        kv_copy(1, 1, n, partner, 0).start()
        if n == 0:
            w_in[2].wait()
        made = jnp.dot(x, wv[0], preferred_element_type=jnp.float32) + bias_of(0)
        for g in range(heads):
            cols = slice(g * HD, (g + 1) * HD)
            piece = normed(made[:, cols], 0).astype(jnp.bfloat16)
            at = 0
            for _, _, rows, block, start in pieces:
                qb[block, start : start + rows, cols] = piece[at : at + rows]
                at += rows

    def relay(n):
        kv_wait(0, n, c, 1)
        kv_copy(0, 0, n, partner, 3).start()
        kv_wait(2, n, c, 2)
        kv_copy(2, 2, n, partner, 4).start()

    def near(n):
        kv_wait(1, n, 1 - c, 0)

    def far(n):
        kv_wait(0, n, 1 - c, 3)
        kv_wait(2, n, 1 - c, 4)

    own_in.wait()
    small[0].wait()
    small[1].wait()
    project(0)
    small[2].wait()
    small[3].wait()

    def check_row(t, bad):
        n = counts[t]
        for s in range(slots):
            gap = lax.rem(lists[s, t] // 4 - t // 4 + n_z, n_z)
            far_one = jnp.where((gap > 1) & (gap < n_z - 1) & (s < n), 1, 0)
            bad = jnp.maximum(bad, far_one)
        return bad

    bad = lax.fori_loop(0, n_tiles, check_row, jnp.int32(0))
    flags[0] = jnp.full(flags.shape[1:], bad, jnp.int32)

    def mask_entry(i, carry):
        q = i // 12
        f = lax.rem(i // 4, 3)
        kt = lax.rem(i // 2, 2)
        core = lax.rem(i, 2)
        row = 2 * b + lax.rem(t0 + q, 2)
        tile = 4 * lax.rem(z + f + n_z - 1, n_z) + 2 * core + lax.rem(t0 + kt, 2)
        n = counts[row]
        hit = jnp.int32(0)
        for s in range(slots):
            hit = jnp.maximum(hit, jnp.where((lists[s, row] == tile) & (s < n), 1, 0))
        mask[i] = hit.astype(jnp.float32)
        return carry

    lax.fori_loop(0, 24, mask_entry, 0)

    def flag_send(src, dst, to, k):
        return pltpu.make_async_remote_copy(
            src_ref=flags.at[src],
            dst_ref=flags.at[dst],
            send_sem=fs_sem.at[k],
            recv_sem=fr_sem.at[k],
            device_id={"dp": to},
            device_id_type=MESH,
        )

    flag_sends = [flag_send(0, 1, d_up, 0), flag_send(0, 2, d_down, 1), flag_send(3, 4, d_up, 2)]
    flag_sends[0].start()
    flag_sends[1].start()

    def flag_wait(dst, k):
        ref = flags.at[dst]
        pltpu.make_async_copy(ref, ref, fr_sem.at[k]).wait()

    acc[...] = jnp.zeros_like(acc)

    mixed = [(half, 1 - mate_left), (half, mate_left)]
    segments = [[(chunk, 0)], mixed, mixed, [(2 * part, 1)], [(2 * rest, 1)]]

    def attend(block, count, tile, groups, joined=False):
        spans = []
        for f, group in groups:
            base = tile * 12 + f * 4
            live = jnp.concatenate(
                [
                    jnp.full((rows, HD), mask[base + kt * 2 + core], jnp.float32)
                    for n in group
                    for core in range(2)
                    for rows, kt in segments[n]
                ],
                axis=0,
            ).astype(jnp.bfloat16)
            first = batches[group[0]][0]
            spans.append((f, slice(first, first + live.shape[0]), live))
        rows = pl.ds(block, count)
        for g in range(heads):
            qh = qb[rows, :, g * HD : (g + 1) * HD].reshape(count * chunk, HD)
            pieces = [
                (
                    kv[f, keys, g * HD : (g + 1) * HD],
                    jnp.concatenate(
                        [kv[f, keys, width + g * HD : width + (g + 1) * HD] * live, live], axis=1
                    ),
                )
                for f, keys, live in spans
            ]
            if joined:
                pieces = [tuple(jnp.concatenate(part, axis=0) for part in zip(*pieces))]
            added = None
            for kh, ext in pieces:
                score = lax.dot_general(
                    qh, kh, (((1,), (1,)), ((), ())), preferred_element_type=jnp.float32
                )
                w = jnp.exp(score * HD ** (-0.5)).astype(jnp.bfloat16)
                term = jnp.dot(w, ext, preferred_element_type=jnp.float32)
                added = term if added is None else added + term
            acc[rows, g] += added.reshape(count, chunk, 2 * HD)

    def finish(block):
        for g in range(heads):
            full = acc[block, g]
            ob[block, :, g * HD : (g + 1) * HD] = (full[:, :HD] / full[:, HD:]).astype(jnp.bfloat16)

    def columns(p):
        return pl.ds(pl.multiple_of(p * width, width), width)

    def out_send(src, dst, to, k):
        return pltpu.make_async_remote_copy(
            src_ref=src,
            dst_ref=dst,
            send_sem=os_sem.at[k],
            recv_sem=or_sem.at[k],
            device_id={"head": to},
            device_id_type=MESH,
        )

    upper, lower = pl.ds(0, half), pl.ds(half, half)
    out_sends = [
        out_send(ob.at[3, upper], passing.at[0], right, 0),
        out_send(ob.at[3, lower], passing.at[1], left, 1),
        out_send(ob.at[2], out.at[:, columns(h)], other, 2),
        out_send(ob.at[1], out.at[:, columns(h)], mate, 3),
        out_send(passing.at[0], out.at[upper, columns(left)], right, 4),
        out_send(passing.at[1], out.at[lower, columns(right)], left, 5),
    ]
    own_out = pltpu.make_async_copy(ob.at[0], out.at[:, columns(h)], own_sem)

    hid_wait(1, 0, half, 0)
    hops[4].start()
    hops[6].start()
    hid_wait(2, half, half, 4)
    hops[5].start()
    hops[7].start()
    relay(0)
    project(1)
    flag_wait(1, 0)
    flags[3] = jnp.maximum(flags[0], flags[1])
    flag_sends[2].start()
    near(0)
    near(1)

    def own_first(i, carry):
        @pl.when(i == 1)
        def _():
            relay(1)
            far(0)
            far(1)

        attend(0, 1, 0, [(lax.rem(2 * i + 1, 3), (0, 1))])
        return carry

    lax.fori_loop(0, 3, own_first, 0)
    flag_wait(2, 1)
    flag_wait(4, 2)
    seen = jnp.maximum(jnp.maximum(flags[2], flags[3]), flags[4])
    flag_out[...] = seen[0:1, 0:1]
    hid_wait(1, half, half, 1)
    hid_wait(2, 0, half, 5)
    project(2)

    def neighbours_first(i, carry):
        attend(1 + i, 1, i, [(f, (0, 1)) for f in range(3)])
        return carry

    lax.fori_loop(0, 2, neighbours_first, 0)
    near(2)
    attend(0, 2, 0, [(1, (2,))])
    attend(2, 1, 1, [(1, (2,))])
    hid_wait(3, 0, part, 2)
    hid_wait(3, chunk - part, part, 6)
    project(3)
    relay(2)
    far(2)
    attend(0, 2, 0, [(0, (2,)), (2, (2,))], True)
    attend(2, 1, 1, [(0, (2,)), (2, (2,))], True)
    hid_wait(3, part, rest, 3)
    hid_wait(3, half, rest, 7)
    project(4)
    attend(3, 1, 1, [(f, (0, 1)) for f in range(3)])
    keep = [pltpu.make_async_copy(qb, q_out, x_sem.at[5])]
    at = 0
    for n, (_, rows, _) in enumerate(batches):
        keep.append(pltpu.make_async_copy(kv.at[1, key_rows(n, c)], kv_out.at[pl.ds(at, rows)], x_sem.at[n]))
        at += rows
    relay(3)
    attend(3, 1, 1, [(f, (2,)) for f in range(3)], True)
    near(3)
    far(3)
    relay(4)
    attend(2, 2, 1, [(f, (3,)) for f in range(3)], True)
    near(4)
    far(4)
    attend(2, 2, 1, [(f, (4,)) for f in range(3)], True)
    finish(3)
    out_sends[0].start()
    out_sends[1].start()
    finish(2)
    out_sends[2].start()
    attend(0, 2, 0, [(f, (3, 4)) for f in range(3)], True)
    finish(1)
    out_sends[3].start()
    finish(0)
    own_out.start()
    for copy in keep:
        copy.start()
    for k in range(2):
        ref = passing.at[k]
        pltpu.make_async_copy(ref, ref, or_sem.at[k]).wait()
        out_sends[4 + k].start()

    for copy in hops:
        copy.wait_send()
    for n in range(5):
        kv_copy(1, 1, n, partner, 0).wait_send()
        kv_copy(1, 0, n, up, 1).wait_send()
        kv_copy(1, 2, n, down, 2).wait_send()
        kv_copy(0, 0, n, partner, 3).wait_send()
        kv_copy(2, 2, n, partner, 4).wait_send()
    for copy in flag_sends:
        copy.wait_send()
    for copy in keep:
        copy.wait()
    own_out.wait()
    for copy in out_sends:
        copy.wait_send()
    for k, ref in (
        (2, out.at[:, columns(other)]),
        (3, out.at[:, columns(mate)]),
        (4, out.at[upper, columns(opp)]),
        (5, out.at[lower, columns(opp)]),
    ):
        pltpu.make_async_copy(ref, ref, or_sem.at[k]).wait()


def window_attention(hidden, weight, bias, gains, lists, counts):
    n_blk = lax.axis_size("blk")
    n_dp = lax.axis_size("dp")
    chunk, depth = hidden.shape
    width = weight.shape[2]
    heads = width // HD
    slots, n_tiles = lists.shape
    sizes = (n_blk, n_dp, heads, slots, n_tiles)
    hbm = pl.BlockSpec(memory_space=pl.ANY)
    vmem = pl.BlockSpec(memory_space=pltpu.VMEM)
    dma = pltpu.SemaphoreType.DMA
    return pl.pallas_call(
        functools.partial(kernel, sizes),
        out_shape=(
            jax.ShapeDtypeStruct((chunk, 4 * width), jnp.bfloat16),
            jax.ShapeDtypeStruct((4, chunk, width), jnp.bfloat16),
            jax.ShapeDtypeStruct((4 * chunk, 2 * width), jnp.bfloat16),
            jax.ShapeDtypeStruct((1, 1), jnp.int32),
        ),
        in_specs=[hbm] * 6,
        out_specs=(hbm, hbm, hbm, vmem),
        scratch_shapes=[
            pltpu.VMEM((4, chunk, depth), jnp.bfloat16),
            pltpu.VMEM((3, depth, width), jnp.bfloat16),
            pltpu.VMEM((4, chunk, width), jnp.bfloat16),
            pltpu.VMEM((3, 8 * chunk, 2 * width), jnp.bfloat16),
            pltpu.VMEM((4, heads, chunk, 2 * HD), jnp.float32),
            pltpu.VMEM((4, chunk, width), jnp.bfloat16),
            pltpu.VMEM((2, chunk // 2, width), jnp.bfloat16),
            pltpu.VMEM((5, 8, 128), jnp.int32),
            pltpu.SMEM((24,), jnp.float32),
            pltpu.VMEM(bias.shape, bias.dtype),
            pltpu.VMEM(gains.shape, gains.dtype),
            pltpu.SMEM(lists.shape, lists.dtype),
            pltpu.SMEM(counts.shape, counts.dtype),
            dma,
            dma((3,)),
            dma((8,)),
            dma((8,)),
            dma((5, 5)),
            dma((5, 5)),
            dma((6,)),
            dma((6,)),
            dma((3,)),
            dma((3,)),
            dma((6,)),
            dma((4,)),
        ],
        compiler_params=pltpu.CompilerParams(
            collective_id=0, has_side_effects=True, vmem_limit_bytes=60 * 1024 * 1024
        ),
    )(hidden, weight, bias, gains, lists, counts)


def any_lists(query, key_value, tile_lists, tile_counts):
    n_blk = lax.axis_size("blk")
    place = lax.axis_index("blk")
    h = lax.axis_index("head")
    chunk, width = query.shape[1:]
    heads = width // HD
    rows = 2 * TILE
    half, part = chunk // 2, chunk // 3

    def in_order(own, right, opposite, left):
        around = jnp.concatenate([own, right, opposite, left] * 2, axis=0)
        return lax.dynamic_slice_in_dim(around, lax.rem(4 - h, 4) * chunk, rows, 0)

    odd = lax.rem(h, 2) == 1
    right_q = jnp.where(odd, query[2], query[1])
    left_q = jnp.where(odd, query[1], query[2])
    query = in_order(query[0], right_q, query[3], left_q).reshape(rows, heads, HD)
    one, two, opp = (key_value[i * chunk : (i + 1) * chunk] for i in (1, 2, 3))
    current = in_order(
        key_value[:chunk],
        jnp.concatenate([two[half:], one[half:]], axis=0),
        jnp.concatenate([opp[:part], opp[2 * part :], opp[part : 2 * part]], axis=0),
        jnp.concatenate([one[:half], two[:half]], axis=0),
    )
    lists = lax.dynamic_slice_in_dim(tile_lists, place * 2, 2, 0)
    counts = lax.dynamic_slice_in_dim(tile_counts, place * 2, 2, 0)
    live = jnp.arange(lists.shape[1], dtype=jnp.int32)[None, :] < counts[:, None]
    route = [(i, (i - 1) % n_blk) for i in range(n_blk)]

    def turn(step, carry):
        total, numer, block = carry
        key_tile = 2 * ((place + step) % n_blk) + jnp.arange(rows, dtype=jnp.int32) // TILE
        hits = (lists[:, :, None] == key_tile[None, None, :]) & live[:, :, None]
        mask = jnp.repeat(jnp.any(hits, axis=1), TILE, axis=0)
        keys = block[:, :width].reshape(rows, heads, HD)
        values = block[:, width:].reshape(rows, heads, HD)
        score = jnp.einsum("qhd,khd->hqk", query, keys, preferred_element_type=jnp.float32)
        w = jnp.where(mask[None], jnp.exp(score * HD ** (-0.5)), jnp.float32(0.0))
        total = total + jnp.sum(w, axis=-1)
        numer = numer + jnp.einsum(
            "hqk,khd->hqd", w.astype(jnp.bfloat16), values, preferred_element_type=jnp.float32
        )
        return (total, numer, lax.ppermute(block, "blk", route))

    total, numer, current = lax.fori_loop(
        0,
        n_blk,
        turn,
        (
            jnp.zeros((heads, rows), jnp.float32),
            jnp.zeros((heads, rows, HD), jnp.float32),
            current,
        ),
    )
    attended = (numer / total[:, :, None]).transpose(1, 0, 2).reshape(rows, width)
    return lax.all_to_all(
        attended.astype(jnp.bfloat16), "head", split_axis=0, concat_axis=1, tiled=True
    )


def shards(hidden, qkv_weight, qkv_bias, norm_gains, tile_lists, tile_counts):
    out, query, key_value, flag = window_attention(
        hidden, qkv_weight, qkv_bias, norm_gains, tile_lists.T, tile_counts
    )
    return lax.cond(
        flag[0, 0] > 0,
        lambda: any_lists(query, key_value, tile_lists, tile_counts),
        lambda: out,
    )


def solution(mesh):
    return jax.shard_map(
        shards,
        mesh=mesh,
        in_specs=(
            P(("dp", "blk", "head"), None),
            P(None, None, "head"),
            P(None, "head"),
            P(),
            P("dp", None),
            P("dp"),
        ),
        out_specs=P(("dp", "blk", "head"), None),
        check_vma=False,
    )
```
